32 devices in a mesh: groups: 2 (over y), tiles: 8 (over z, core), ens: 2 (over x), lev: 1.
Axes of the slice: x: 2, y: 2, z: 4, core: 2. Of those that a mesh axis runs over, the one named last changes fastest.
Arguments:
- inputs: bfloat16 [2, 1, 16, 3, 32, 32, 128], P('ens', 'lev', ('groups', 'tiles')), parts along dimension 2, may hold values from -6 to 6
- slot_rows: int32 [16, 3], P('groups'), parts along dimension 0, may hold values from -1 to 3, as said below
- cell_mask: int32 [1, 16, 3, 32, 32], P('lev', ('groups', 'tiles')), parts along dimension 1, may hold values 0 or 1
- target: bfloat16 [1, 16, 3, 4, 32, 32], P('lev', ('groups', 'tiles')), parts along dimension 1, may hold values from -24 to 24
- dw_kernel: float32 [7, 7, 128], replicated, may hold values from -0.875 to 0.875
- dw_bias: float32 [128], replicated, may hold values from -3 to 3
- ln_gain: float32 [128], replicated, may hold values from 0.1 to 1.9
- ln_bias: float32 [128], replicated, may hold values from -3 to 3
- w_in: bfloat16 [128, 256], replicated, may hold values from -0.5 to 0.5
- b_in: float32 [256], replicated, may hold values from -3 to 3
- w_out: bfloat16 [256, 128], replicated, may hold values from -0.375 to 0.375
- b_out: float32 [128], replicated, may hold values from -3 to 3
- layer_scale: float32 [128], replicated, may hold values from 0.3 to 1.5
- w_head: float32 [128, 4], replicated, may hold values from -2 to 2
Outputs:
- grad_x: bfloat16 [2, 1, 16, 3, 32, 32, 128], P('ens', 'lev', ('groups', 'tiles')), parts along dimension 2
- crps: bfloat16 [1, 16, 3, 32, 32], P('lev', ('groups', 'tiles'), None, 'ens'), parts along dimension 1
The draws below stay inside these ranges and needn't reach their ends.
There are 2 independent parts, one for each index of `groups`. The reference program is written for one: setup_inputs(seed, part) draws one part's arguments, and reference() takes and returns one part's arrays. A program takes and returns all parts, laid end to end along the dimension named above; an argument that names none is the same for every part. Nothing has to cross between parts.
Inputs may be any that keep to these rules, and one draw needn't show every extreme that they name: `slot_rows`: each row c lists the tile rows of the ocean tiles of tile column c in increasing order, each at most once, followed by -1 in the empty slots. Tile columns c and c + 4 hold 4 ocean tiles together; every column holds 1 to 3, and some column holds exactly 3.
All inputs are finite; a program needn't handle non-finite values. No bound on the sum of `cell_mask` on one device may be relied on, other than what follows from the above.
Results may differ from the reference program's by a relative error of at most 0.012.
Values may be sent and summed in bfloat16 or wider, within the bound.
A program may use at most 64 MiB of HBM per device.

```python
import math
import jax
import jax.numpy as jnp
from jax import lax

C = 128
HID = 256
NV = 4
KERNEL = 7
TILE = 32
PAIR_TILES = 4
SLOTS = 3
COLS = 8
MEMBERS = 2
LEVELS = 1


def draw_slot_rows(key, part):
    half_cols = COLS // 2
    key_count, key_pick, key_side, key_rows = jax.random.split(key, 4)
    counts_low = jax.random.randint(key_count, (half_cols,), 1, PAIR_TILES)
    chosen = jax.random.randint(key_pick, (), 0, half_cols)
    side = jax.random.randint(key_side, (), 0, 2)
    forced = jnp.where(side == 0, PAIR_TILES - 1, 1)
    counts_low = jnp.where(jnp.arange(half_cols) == chosen, forced, counts_low)
    counts = jnp.concatenate([counts_low, PAIR_TILES - counts_low])

    def shuffled(row_key):
        return jax.random.permutation(row_key, PAIR_TILES)
    order = jax.vmap(shuffled)(jax.random.split(key_rows, COLS))
    position = jnp.argsort(order, axis=1)
    selected = position < counts[:, None]
    row_ids = jnp.arange(PAIR_TILES, dtype=jnp.int32)[None, :]
    keyed = jnp.where(selected, row_ids, PAIR_TILES + row_ids)
    ordered = jnp.sort(keyed, axis=1)[:, :PAIR_TILES - 1]
    return jnp.where(ordered < PAIR_TILES, ordered, -1).astype(jnp.int32)


def touch_ends(entries, stream_key, low, largest):
    longest = entries.shape.index(max(entries.shape))
    spots = []
    for shift in (0, 1):
        where = [jax.random.randint(jax.random.fold_in(stream_key, axis), (), 0, length) for axis, length in enumerate(entries.shape)]
        where[longest] = (where[longest] + shift) % entries.shape[longest]
        spots.append(tuple(where))
    return entries.at[spots[0]].set(low).at[spots[1]].set(largest)


def block_levels(own_key, extent, cuts, least, top_value):
    def one(axis_at, shards_of):
        heights = jax.random.uniform(jax.random.fold_in(jax.random.fold_in(own_key, 6), axis_at), (shards_of,), jnp.float32, least / len(cuts), top_value / len(cuts))
        return jnp.repeat(jnp.exp(heights), extent[axis_at] // shards_of).reshape((-1,) + (1,) * (len(extent) - axis_at - 1))

    gain = one(*cuts[0])
    for cut in cuts[1:]:
        gain = gain * one(*cut)
    return gain


def gaussian(own_key, extent, scale, limit, cuts=(), kind=jnp.bfloat16):
    loudness = block_levels(own_key, extent, cuts, -0.22, 0.18) if cuts else 1.0
    array = jax.random.normal(own_key, extent, jnp.float32) * scale * loudness
    return jnp.minimum(jnp.maximum(array, -limit), limit).astype(kind)


def setup_inputs(seed: int = 0, part: int = 0) -> dict:
    arg_keys = jax.random.split(jax.random.key(seed), 15)
    own_keys = jax.random.split(jax.random.fold_in(arg_keys[14], part), 15)
    inputs = gaussian(own_keys[0], (MEMBERS, LEVELS, COLS, SLOTS, TILE, TILE, C), 1.0, 6.0, ((0, 2), (2, 8)))
    slot_rows = draw_slot_rows(jax.random.fold_in(jax.random.fold_in(arg_keys[14], part), 71), part)
    cell_mask = touch_ends((jax.random.randint(own_keys[2], (LEVELS, COLS, SLOTS, TILE, TILE), 0, 8) < 7).astype(jnp.int32), jax.random.fold_in(own_keys[2], 1), 0, 1)
    target = gaussian(own_keys[3], (LEVELS, COLS, SLOTS, NV, TILE, TILE), 4.0, 24.0, ((1, 8),))
    dw_kernel = gaussian(arg_keys[4], (KERNEL, KERNEL, C), (KERNEL * KERNEL) ** -0.5, 0.875, (), jnp.float32)
    dw_bias = gaussian(arg_keys[5], (C,), 0.5, 3.0, (), jnp.float32)
    ln_gain = jnp.clip(1.0 + 0.18 * jax.random.normal(arg_keys[6], (C,), jnp.float32), 0.1, 1.9)
    ln_bias = gaussian(arg_keys[7], (C,), 0.5, 3.0, (), jnp.float32)
    w_in = gaussian(arg_keys[8], (C, HID), C ** -0.5, 0.5)
    b_in = gaussian(arg_keys[9], (HID,), 0.5, 3.0, (), jnp.float32)
    w_out = gaussian(arg_keys[10], (HID, C), HID ** -0.5, 0.375)
    b_out = gaussian(arg_keys[11], (C,), 0.5, 3.0, (), jnp.float32)
    layer_scale = jnp.clip(jnp.exp(jax.random.uniform(arg_keys[12], (C,), jnp.float32, math.log(0.3), math.log(1.5))), 0.3, 1.5)
    w_head = gaussian(arg_keys[13], (C, NV), 0.35, 2.0, (), jnp.float32)
    return {"inputs": inputs, "slot_rows": slot_rows, "cell_mask": cell_mask, "target": target, "dw_kernel": dw_kernel, "dw_bias": dw_bias, "ln_gain": ln_gain, "ln_bias": ln_bias, "w_in": w_in, "b_in": b_in, "w_out": w_out, "b_out": b_out, "layer_scale": layer_scale, "w_head": w_head}


softness = 0.0625
epsilon = 1e-06
highest = lax.Precision.HIGHEST

def soft_abs(value):
    return jnp.sqrt(value * value + softness)

def soft_sign(value):
    return value / jnp.sqrt(value * value + softness)

def gelu_slope(value):
    cumulative = 0.5 * (1.0 + lax.erf(value * 0.7071067811865476))
    return cumulative + value * jnp.exp(-0.5 * value * value) * 0.3989422804014327

def place_grid(tiles, onehot):
    placed = jnp.einsum('csr,csabk->rcabk', onehot, tiles, precision=highest)
    grid_rows = placed.shape[0]
    columns = placed.shape[1]
    tile = placed.shape[2]
    width = placed.shape[4]
    return placed.transpose(0, 2, 1, 3, 4).reshape(grid_rows * tile, columns * tile, width)

def take_grid(grid, onehot, tile):
    grid_rows = onehot.shape[2]
    columns = onehot.shape[0]
    width = grid.shape[2]
    blocks = grid.reshape(grid_rows, tile, columns, tile, width).transpose(0, 2, 1, 3, 4)
    return jnp.einsum('csr,rcabk->csabk', onehot, blocks, precision=highest)

def stencil_grid(grid, weights):
    size = weights.shape[0]
    rim = size // 2
    padded = jnp.pad(grid, ((rim, rim), (0, 0), (0, 0)))
    padded = jnp.concatenate([padded[:, padded.shape[1] - rim:], padded, padded[:, :rim]], axis=1)
    height = grid.shape[0]
    breadth = grid.shape[1]
    total = jnp.zeros(grid.shape, jnp.float32)
    for row_off in range(size):
        for col_off in range(size):
            total = total + weights[row_off, col_off] * padded[row_off:row_off + height, col_off:col_off + breadth]
    return total

def reference(inputs, slot_rows, cell_mask, target, dw_kernel, dw_bias, ln_gain, ln_bias, w_in, b_in, w_out, b_out, layer_scale, w_head):
    members = inputs.shape[0]
    levels = inputs.shape[1]
    columns = inputs.shape[2]
    slots = inputs.shape[3]
    tile = inputs.shape[4]
    width = inputs.shape[6]
    live = (slot_rows >= 0).astype(jnp.float32)
    onehot = (slot_rows[:, :, None] == jnp.arange(PAIR_TILES, dtype=jnp.int32)[None, None, :]).astype(jnp.float32)
    weight_mask = cell_mask.astype(jnp.float32) * live[None, :, :, None, None]
    flipped = dw_kernel[::-1, ::-1]

    def forward(tiles, mask):
        masked_x = tiles.astype(jnp.float32) * mask[..., None]
        conv_out = take_grid(stencil_grid(place_grid(masked_x, onehot), dw_kernel), onehot, tile) + dw_bias
        mean_z = lax.optimization_barrier(jnp.mean(conv_out, axis=-1, keepdims=True))
        centered = conv_out - mean_z
        inv_std = lax.rsqrt(lax.optimization_barrier(jnp.mean(centered * centered, axis=-1, keepdims=True)) + epsilon)
        normed = centered * inv_std
        features = (normed * ln_gain + ln_bias).astype(jnp.bfloat16)
        pre = jnp.dot(features.reshape(-1, width), w_in, preferred_element_type=jnp.float32) + b_in
        act = jax.nn.gelu(pre, approximate=False).astype(jnp.bfloat16)
        branch = jnp.dot(act, w_out, preferred_element_type=jnp.float32) + b_out
        pred = jnp.dot(masked_x.reshape(-1, width), w_head, precision=highest) + jnp.dot(layer_scale * branch, w_head, precision=highest)
        pred = pred.reshape(columns, slots, tile, tile, NV).transpose(0, 1, 4, 2, 3)
        return (pred, inv_std, normed, pre)
    flat_x = inputs.reshape((members * levels,) + inputs.shape[2:])
    flat_mask = jnp.broadcast_to(weight_mask[None], (members,) + weight_mask.shape).reshape((members * levels,) + weight_mask.shape[1:])

    def forward_pred(pair):
        return forward(pair[0], pair[1])[0]
    preds = lax.map(forward_pred, (flat_x, flat_mask)).reshape((members, levels) + (columns, slots, NV, tile, tile))
    observed = target.astype(jnp.float32)
    mask_var = weight_mask[:, :, :, None]
    skill = jnp.zeros(observed.shape, jnp.float32)
    spread = jnp.zeros(observed.shape, jnp.float32)
    for first in range(members):
        skill = skill + soft_abs(preds[first] - observed)
        for second in range(members):
            spread = spread + soft_abs(preds[first] - preds[second])
    skill = skill / members
    spread = spread / (2 * members * members)
    crps = (weight_mask * lax.optimization_barrier(jnp.sum(skill - spread, axis=3))).astype(jnp.bfloat16)
    grads = []
    for first in range(members):
        pair_sum = jnp.zeros(observed.shape, jnp.float32)
        for second in range(members):
            pair_sum = pair_sum + soft_sign(preds[first] - preds[second])
        grads.append((mask_var * (soft_sign(preds[first] - observed) / members - pair_sum / (members * members))).astype(jnp.bfloat16))
    grad_pred = jnp.stack(grads).reshape((members * levels,) + observed.shape[1:])

    def backward(triple):
        tiles, mask, grad_one = triple
        pred, inv_std, normed, pre = forward(tiles, mask)
        grad_rows = jnp.dot(grad_one.astype(jnp.float32).transpose(0, 1, 3, 4, 2).reshape(-1, NV), w_head.T, precision=highest)
        scaled = (layer_scale * grad_rows).astype(jnp.bfloat16)
        grad_act = jnp.dot(scaled, w_out.T, preferred_element_type=jnp.float32)
        grad_pre = (grad_act * gelu_slope(pre)).astype(jnp.bfloat16)
        grad_feat = jnp.dot(grad_pre, w_in.T, preferred_element_type=jnp.float32).astype(jnp.bfloat16)
        gated = grad_feat.astype(jnp.float32).reshape(normed.shape) * ln_gain
        grad_z = (inv_std * (gated - lax.optimization_barrier(jnp.mean(gated, axis=-1, keepdims=True)) - normed * lax.optimization_barrier(jnp.mean(gated * normed, axis=-1, keepdims=True)))).astype(jnp.bfloat16)
        through = take_grid(stencil_grid(place_grid(grad_z.astype(jnp.float32), onehot), flipped), onehot, tile)
        return (mask[..., None] * (grad_rows.reshape(normed.shape) + through)).astype(jnp.bfloat16)
    grad_x = lax.map(backward, (flat_x, flat_mask, grad_pred)).reshape(inputs.shape)
    return (grad_x, crps)
```

```python
import functools

import jax
import jax.numpy as jnp
from jax import lax
from jax.experimental import pallas as pl
from jax.experimental.pallas import tpu as pltpu
from jax.sharding import PartitionSpec as P

softness = 0.0625
epsilon = 1e-06
MESH = pl.DeviceIdType.MESH
f32 = jnp.float32
bf16 = jnp.bfloat16
LEFT = 8
NT = (((1,), (1,)), ((), ()))
TN = (((0,), (0,)), ((), ()))


def soft_abs(value):
    return jnp.sqrt(value * value + softness)


def soft_sign(value):
    return value * lax.rsqrt(value * value + softness)


def kernel(
    members,
    columns,
    rows_ref,
    x_ref,
    mask_ref,
    goal_ref,
    dw_ref,
    dwb_ref,
    gain_ref,
    lnb_ref,
    win_ref,
    bin_ref,
    wout_ref,
    bout_ref,
    ls_ref,
    wh_ref,
    out_ref,
    crps_ref,
    pad,
    lhs,
    taps,
    band,
    acc,
    normed,
    invs,
    grows,
    mcol,
    xm,
    feat,
    pre,
    act,
    slope,
    flat,
    goals,
    masks,
    shuffle,
    halo,
    ex,
    hx,
    eg,
    hg,
    pmine,
    pall,
    sx,
    rx,
    sg,
    rg,
    sp,
    rp,
    *,
    slots,
    tile,
    size,
    nv,
):
    rim = size // 2
    half = tile // 2
    width = x_ref.shape[-1]
    lanes = width // 2
    cells = tile * tile
    group = width // tile
    depth = (size + 1) // 2
    me = lax.axis_index("tiles")
    mine = lax.axis_index("ens")
    west = lax.rem(me + columns - 1, columns)
    east = lax.rem(me + 1, columns)

    barrier = pltpu.get_barrier_semaphore()
    pl.semaphore_signal(barrier, inc=1, device_id={"tiles": west}, device_id_type=MESH)
    pl.semaphore_signal(barrier, inc=1, device_id={"tiles": east}, device_id_type=MESH)
    for p in range(1, members):
        pl.semaphore_signal(
            barrier, inc=1, device_id={"ens": lax.rem(mine + p, members)}, device_id_type=MESH
        )

    zero_strip = jnp.zeros((rim, tile, width), bf16)
    for side in range(2):
        hx[side, slots] = zero_strip
        hg[side, slots] = zero_strip

    eye_tile = (
        lax.broadcasted_iota(jnp.int32, (tile, tile), 0)
        == lax.broadcasted_iota(jnp.int32, (tile, tile), 1)
    ).astype(f32)
    ones = jnp.ones((tile, width), bf16)

    def mask_slot(s, carry):
        live = (rows_ref[s, me] >= 0).astype(f32)
        m = mask_ref[s].astype(f32) * live
        flat[nv * tile : (nv + 1) * tile, :tile] = m
        spread = (m[:, None, :] * eye_tile[None]).reshape(cells, tile).astype(bf16)
        col = jnp.dot(spread, ones, preferred_element_type=f32)
        mcol[s] = col
        xv = x_ref[s].astype(f32).reshape(cells, width) * col
        xm[s] = xv.astype(bf16)
        x3 = xv.reshape(tile, tile, width)
        edge = jnp.zeros((tile, LEFT, width), f32)
        pad[s, :, LEFT : LEFT + tile, :] = x3
        pad[s, :, 0:LEFT, :] = edge
        pad[s, :, LEFT + tile : LEFT + tile + 8, :] = edge
        flat[0 : nv * tile, :tile] = goal_ref[s].astype(f32).reshape(nv * tile, tile)
        lane = lax.broadcasted_iota(jnp.int32, (tile // group, width), 1)
        for v in range(nv + 1):
            total = None
            for r in range(group):
                piece = flat[pl.ds(v * tile + r, tile // group, stride=group), :]
                if r:
                    piece = pltpu.roll(piece, r * tile, 1)
                total = piece if r == 0 else jnp.where(lane >= r * tile, piece, total)
            if v < nv:
                goals[s, v] = total
            else:
                masks[s] = total
        return carry

    def strips(s, dst):
        for c in range(rim):
            dst[0, s, c] = pad[s, :, LEFT + tile - rim + c, :].astype(bf16)
            dst[1, s, c] = pad[s, :, LEFT + c, :].astype(bf16)

    lax.fori_loop(0, slots, mask_slot, 0)
    for s in range(slots):
        strips(s, ex)

    pl.semaphore_wait(barrier, 2 + members - 1)

    def edge_copy(src, dst, send, recv, side):
        return pltpu.make_async_remote_copy(
            src_ref=src,
            dst_ref=dst,
            send_sem=send,
            recv_sem=recv,
            device_id={"tiles": east if side == 0 else west},
            device_id_type=MESH,
        )

    x_copies = [
        edge_copy(ex.at[side], hx.at[side, pl.ds(0, slots)], sx.at[side], rx.at[side], side)
        for side in range(2)
    ]
    for copy in x_copies:
        copy.start()

    low = lax.broadcasted_iota(jnp.int32, (8, width), 1) < lanes
    zero_row = jnp.zeros((1, width), f32)
    for part in range(2):
        taps[part, 0] = jnp.zeros((8, width), f32)
        taps[part, size + 1] = jnp.zeros((8, width), f32)
    for i in range(size):
        now = jnp.concatenate([dw_ref[i], zero_row], axis=0)
        before = jnp.concatenate([zero_row, dw_ref[i]], axis=0)
        taps[0, i + 1] = jnp.where(low, now, pltpu.roll(before, lanes, 1))
        taps[1, i + 1] = jnp.where(low, pltpu.roll(now, lanes, 1), before)

    diagonal = lax.rem(lax.broadcasted_iota(jnp.int32, (lanes, width), 1), lanes) == (
        lax.broadcasted_iota(jnp.int32, (lanes, width), 0)
    )

    def build_band(t, carry):
        part = t // (depth * depth)
        dy = lax.rem(t // depth, depth)
        dx = lax.rem(t, depth)
        for py in range(2):
            for px in range(2):
                for qy in range(2):
                    row = taps[part, 1 + 2 * dy + py - qy, pl.ds(2 * dx + px, 1), :]
                    block = jnp.where(diagonal, jnp.broadcast_to(row, (lanes, width)), 0.0)
                    at = (2 * py + px) * lanes
                    band[t, at : at + lanes, qy * width : (qy + 1) * width] = block.astype(bf16)
        return carry

    lax.fori_loop(0, 2 * depth * depth, build_band, 0)

    scaled_head = wh_ref[...] * ls_ref[...]
    through_head = lax.dot_general(
        jnp.concatenate([scaled_head, scaled_head], axis=0), wout_ref[...].astype(f32), NT,
        precision=lax.Precision.HIGHEST, preferred_element_type=f32,
    )[:nv]
    bias_head = jnp.sum(scaled_head * bout_ref[...], axis=1, keepdims=True)
    both = jnp.concatenate([wh_ref[...], through_head], axis=1)
    both_hi = both.astype(bf16).astype(f32)
    both_hl = jnp.concatenate(
        [both_hi, both - both_hi, jnp.zeros((16 - 2 * nv, both.shape[1]), f32)], axis=0
    ).astype(bf16)

    half_lane = lax.broadcasted_iota(jnp.int32, (half, width), 1) < lanes

    def swap(first, second):
        lo = jnp.where(half_lane, first, pltpu.roll(second, lanes, 1))
        hi = jnp.where(half_lane, pltpu.roll(first, lanes, 1), second)
        return lo, hi

    def centre(flip):
        def one(s, carry):
            own = rows_ref[s, me]
            above = jnp.maximum(s - 1, 0)
            below = jnp.minimum(s + 1, slots - 1)
            flag_up = (
                (s > 0) & (own >= 0) & (rows_ref[above, me] == own - 1)
            ).astype(f32)
            flag_down = (
                (s < slots - 1) & (rows_ref[below, me] >= 0) & (rows_ref[below, me] == own + 1)
            ).astype(f32)
            for r in range(tile + 2 * rim):
                y = r - rim
                m, py = r // 2, r % 2
                for dx in range(depth):
                    found = []
                    for px in range(2):
                        at = pl.ds(LEFT - rim + 2 * dx + px, half, stride=2)
                        if y < 0:
                            piece = pad[above, tile + y, at, :] * flag_up
                        elif y >= tile:
                            piece = pad[below, y - tile, at, :] * flag_down
                        else:
                            piece = pad[s, y, at, :]
                        found.append(piece)
                    place = py
                    if flip:
                        found = found[::-1]
                        place = 1 - py
                    lo, hi = swap(*found)
                    lhs[0, dx, m, :, place * width : (place + 1) * width] = lo.astype(bf16)
                    lhs[1, dx, m, :, place * width : (place + 1) * width] = hi.astype(bf16)
            res = []
            for part in range(2):
                left = []
                right = []
                for dy in range(depth):
                    for dx in range(depth):
                        left.append(lhs[part, dx, dy : dy + half].reshape(half * half, 2 * width))
                        oy, ox = (depth - 1 - dy, depth - 1 - dx) if flip else (dy, dx)
                        right.append(band[(part * depth + oy) * depth + ox])
                res.append(
                    jnp.dot(
                        jnp.concatenate(left, axis=1),
                        jnp.concatenate(right, axis=0),
                        preferred_element_type=f32,
                    )
                )
            for qy in range(2):
                y = 1 - qy if flip else qy
                at = slice(qy * width, (qy + 1) * width)
                for k in range(half):
                    rows = slice(k * half, (k + 1) * half)
                    lo, hi = swap(res[0][rows, at], res[1][rows, at])
                    even, odd = (hi, lo) if flip else (lo, hi)
                    acc[s, 2 * k + y, pl.ds(0, half, stride=2), :] = even
                    acc[s, 2 * k + y, pl.ds(1, half, stride=2), :] = odd
            return carry

        lax.fori_loop(0, slots, one, 0)

    def edges(s, buf, flip):
        row = rows_ref[s, me]
        for side, source in ((0, west), (1, east)):
            there = [rows_ref[t, source] for t in range(slots)]

            def find(wanted):
                place = jnp.int32(slots)
                for t in range(slots):
                    place = jnp.where(
                        (there[t] >= 0) & (there[t] == wanted), jnp.int32(t), place
                    )
                return place

            up = find(row - 1)
            level = find(row)
            down = find(row + 1)
            total = [jnp.zeros((tile, width), f32) for _ in range(rim)]
            for c in range(rim):
                halo[side, c, 0:8] = buf[side, up, c].astype(f32)[tile - 8 :]
                halo[side, c, 8 : 8 + tile] = buf[side, level, c].astype(f32)
                halo[side, c, 8 + tile :] = buf[side, down, c].astype(f32)[:8]
                for dy in range(size):
                    piece = halo[side, c, 8 - rim + dy : 8 - rim + dy + tile]
                    for u in range(rim):
                        if (c < u) if side == 0 else (c > u):
                            continue
                        j = c - u if side == 0 else size - 1 + c - u
                        i, j = (size - 1 - dy, size - 1 - j) if flip else (dy, j)
                        total[u] = total[u] + dw_ref[i, j : j + 1, :] * piece
            for u in range(rim):
                col = u if side == 0 else tile - rim + u
                acc[s, :, col, :] = acc[s, :, col, :] + total[u]

    def edges_all(buf, flip):
        def one(s, carry):
            edges(s, buf, flip)
            return carry

        lax.fori_loop(0, slots, one, 0)

    centre(False)
    for copy in x_copies:
        copy.wait()
    edges_all(hx, False)

    strip_rows = 4
    chunk = strip_rows * tile
    small = 64
    nhalf = half * tile

    def pred_copy(s, p):
        return pltpu.make_async_remote_copy(
            src_ref=pmine.at[s],
            dst_ref=pall.at[p - 1, s],
            send_sem=sp.at[p - 1, s],
            recv_sem=rp.at[p - 1, s],
            device_id={"ens": lax.rem(mine + p, members)},
            device_id_type=MESH,
        )

    def forward(s, carry):
        for q in range(tile // strip_rows):
            at = slice(q * chunk, (q + 1) * chunk)
            z = acc[s, q * strip_rows : (q + 1) * strip_rows].reshape(chunk, width) + dwb_ref[...]
            mean = jnp.mean(z, axis=1, keepdims=True)
            z = z - mean
            inv = lax.rsqrt(jnp.mean(z * z, axis=1, keepdims=True) + epsilon)
            z = z * inv
            normed[s, at, :] = z
            invs[s, at, :] = jnp.broadcast_to(inv, (chunk, width))
            feat[at, :] = (z * gain_ref[...] + lnb_ref[...]).astype(bf16)
        for b in range(2):
            base = b * nhalf
            pre[...] = jnp.dot(
                feat[base : base + nhalf, :], win_ref[...], preferred_element_type=f32
            )

            def gelu(q, carry):
                at = pl.ds(pl.multiple_of(q * small, small), small)
                v = pre[at, :] + bin_ref[...]
                cum = 0.5 * (1.0 + lax.erf(v * 0.7071067811865476))
                act[at, :] = (v * cum).astype(bf16)
                slope[s, b, at, :] = cum + v * jnp.exp(-0.5 * v * v) * 0.3989422804014327
                return carry

            lax.fori_loop(0, nhalf // small, gelu, 0, unroll=2)
            r16 = lax.dot_general(
                both_hl,
                jnp.concatenate([xm[s, base : base + nhalf, :], act[...]], axis=1),
                NT,
                preferred_element_type=f32,
            )
            r4 = r16[:nv] + r16[nv : 2 * nv] + bias_head
            for q in range(nhalf // width):
                pmine[s, pl.ds(b * (nhalf // width) + q, nv, stride=cells // width), :] = r4[
                    :, q * width : (q + 1) * width
                ]
        for p in range(1, members):
            pred_copy(s, p).start()
        return carry

    lax.fori_loop(0, slots, forward, 0)

    def gz_copy(s, side):
        return edge_copy(eg.at[side, s], hg.at[side, s], sg.at[side, s], rg.at[side, s], side)

    deep = cells // width

    def backward(s, carry):
        for p in range(1, members):
            pred_copy(s, p).wait()
        every = [pmine[s].reshape(nv, deep, width)] + [
            pall[p - 1, s].reshape(nv, deep, width) for p in range(1, members)
        ]
        goal = goals[s]
        mask = masks[s]
        skill = soft_abs(every[0] - goal)
        spread = jnp.zeros_like(skill)
        pull = jnp.zeros_like(skill)
        for p in range(1, members):
            skill = skill + soft_abs(every[p] - goal)
            pull = pull + soft_sign(every[0] - every[p])
            for other in range(p):
                spread = spread + soft_abs(every[p] - every[other])
        same = members * softness**0.5
        score = mask * jnp.sum(
            skill / members - (2.0 * spread + same) / (2 * members * members), axis=0
        )
        for r in range(group):
            piece = pltpu.roll(score, width - r * tile, 1) if r else score
            shuffle[pl.ds(r, tile // group, stride=group), :] = piece
        share = tile // members
        crps_ref[s] = shuffle[pl.ds(pl.multiple_of(mine * share, share), share), :][:, :tile]
        gp = mask[None] * (
            soft_sign(every[0] - goal) / members - pull / (members * members)
        )
        flat[0 : nv * deep, :] = gp.astype(bf16).astype(f32).reshape(nv * deep, width)
        for b in range(2):
            base = b * nhalf
            g4 = jnp.concatenate(
                [
                    flat[pl.ds(b * (nhalf // width) + q, nv, stride=deep), :]
                    for q in range(nhalf // width)
                ],
                axis=1,
            )
            gp16 = jnp.concatenate(
                [g4, g4, jnp.zeros((16 - 2 * nv, nhalf), f32)], axis=0
            ).astype(bf16)
            big = lax.dot_general(gp16, both_hl, TN, preferred_element_type=f32)
            grows[s, base : base + nhalf, :] = big[:, :width]
            act[...] = (big[:, width:] * slope[s, b]).astype(bf16)
            full = lax.dot_general(act[...], win_ref[...], NT, preferred_element_type=f32)
            for r in range(half):
                at = slice(base + r * tile, base + (r + 1) * tile)
                g = full[r * tile : (r + 1) * tile] * gain_ref[...]
                z = normed[s, at, :]
                g = invs[s, at, :] * (
                    g
                    - jnp.mean(g, axis=1, keepdims=True)
                    - z * jnp.mean(g * z, axis=1, keepdims=True)
                )
                pad[s, b * half + r, LEFT : LEFT + tile, :] = g
        strips(s, eg)
        for side in range(2):
            gz_copy(s, side).start()
        return carry

    lax.fori_loop(0, slots, backward, 0)
    centre(True)
    for s in range(slots):
        for side in range(2):
            gz_copy(s, side).wait()

    def last(s, carry):
        edges(s, hg, True)
        v = mcol[s] * (grows[s] + acc[s].reshape(cells, width))
        out_ref[s] = v.reshape(tile, tile, width).astype(bf16)
        return carry

    lax.fori_loop(0, slots, last, 0)


def on_device(
    inputs,
    slot_rows,
    cell_mask,
    target,
    dw_kernel,
    dw_bias,
    ln_gain,
    ln_bias,
    w_in,
    b_in,
    w_out,
    b_out,
    layer_scale,
    w_head,
):
    columns = lax.axis_size("tiles")
    members = lax.axis_size("ens")
    slots, tile, _, width = inputs.shape[3:]
    size = dw_kernel.shape[0]
    rim = size // 2
    half = tile // 2
    cells = tile * tile
    hidden = w_in.shape[1]
    nv = w_head.shape[1]
    vmem = pl.BlockSpec(memory_space=pltpu.VMEM)
    smem = pl.BlockSpec(memory_space=pltpu.SMEM)
    depth = (size + 1) // 2
    deep = cells // width
    strip = (2, slots, rim, tile, width)
    halo = (2, slots + 1, rim, tile, width)
    dma = pltpu.SemaphoreType.DMA
    grad, score = pl.pallas_call(
        functools.partial(kernel, members, columns, slots=slots, tile=tile, size=size, nv=nv),
        out_shape=(
            jax.ShapeDtypeStruct((slots, tile, tile, width), bf16),
            jax.ShapeDtypeStruct((slots, tile // members, tile), f32),
        ),
        in_specs=[smem] + [vmem] * 13,
        out_specs=(vmem, vmem),
        scratch_shapes=[
            pltpu.VMEM((slots, tile, tile + 16, width), f32),
            pltpu.VMEM((2, depth, half + rim, half, 2 * width), bf16),
            pltpu.VMEM((2, size + 2, 8, width), f32),
            pltpu.VMEM((2 * depth * depth, 2 * width, 2 * width), bf16),
            pltpu.VMEM((slots, tile, tile, width), f32),
            pltpu.VMEM((slots, cells, width), f32),
            pltpu.VMEM((slots, cells, width), f32),
            pltpu.VMEM((slots, cells, width), f32),
            pltpu.VMEM((slots, cells, width), f32),
            pltpu.VMEM((slots, cells, width), bf16),
            pltpu.VMEM((cells, width), bf16),
            pltpu.VMEM((half * tile, hidden), f32),
            pltpu.VMEM((half * tile, hidden), bf16),
            pltpu.VMEM((slots, 2, half * tile, hidden), f32),
            pltpu.VMEM(((nv + 1) * tile, width), f32),
            pltpu.VMEM((slots, nv, deep, width), f32),
            pltpu.VMEM((slots, deep, width), f32),
            pltpu.VMEM((tile, width), f32),
            pltpu.VMEM((2, rim, tile + 16, width), f32),
            pltpu.VMEM(strip, bf16),
            pltpu.VMEM(halo, bf16),
            pltpu.VMEM(strip, bf16),
            pltpu.VMEM(halo, bf16),
            pltpu.VMEM((slots, nv * deep, width), f32),
            pltpu.VMEM((members - 1, slots, nv * deep, width), f32),
            dma((2,)),
            dma((2,)),
            dma((2, slots)),
            dma((2, slots)),
            dma((members - 1, slots)),
            dma((members - 1, slots)),
        ],
        compiler_params=pltpu.CompilerParams(
            collective_id=0, has_side_effects=True, vmem_limit_bytes=60 * 2**20
        ),
    )(
        slot_rows.T,
        inputs.reshape(slots, tile, tile, width),
        cell_mask.reshape(slots, tile, tile),
        target.reshape(slots, nv, tile, tile),
        dw_kernel,
        dw_bias[None],
        ln_gain[None],
        ln_bias[None],
        w_in,
        b_in[None],
        w_out,
        b_out[None],
        layer_scale[None],
        w_head.T,
    )
    return (grad.reshape(inputs.shape), score.astype(bf16)[None, None])


def solution(mesh):
    placed = (
        P("ens", "lev", ("groups", "tiles"), None, None, None, None),
        P("groups", None),
        P("lev", ("groups", "tiles"), None, None, None),
        P("lev", ("groups", "tiles"), None, None, None, None),
    ) + (P(),) * 10
    return jax.shard_map(
        on_device,
        mesh=mesh,
        in_specs=placed,
        out_specs=(
            P("ens", "lev", ("groups", "tiles"), None, None, None, None),
            P("lev", ("groups", "tiles"), None, "ens", None),
        ),
        check_vma=False,
    )
```

```python
import functools

import jax
import jax.numpy as jnp
from jax import lax
from jax.experimental import pallas as pl
from jax.experimental.pallas import tpu as pltpu
from jax.sharding import PartitionSpec as P

softness = 0.0625
epsilon = 1e-06
MESH = pl.DeviceIdType.MESH
f32 = jnp.float32
bf16 = jnp.bfloat16
LEFT = 8
NT = (((1,), (1,)), ((), ()))
TN = (((0,), (0,)), ((), ()))


def soft_abs(value):
    return jnp.sqrt(value * value + softness)


def soft_sign(value):
    return value * lax.rsqrt(value * value + softness)


def kernel(
    members,
    columns,
    rows_hbm,
    x_hbm,
    mask_hbm,
    goal_hbm,
    dw_hbm,
    dwb_hbm,
    gain_hbm,
    lnb_hbm,
    win_hbm,
    bin_hbm,
    wout_hbm,
    bout_hbm,
    ls_hbm,
    wh_hbm,
    out_ref,
    crps_ref,
    pad,
    lhs,
    taps,
    band,
    acc,
    normed,
    invs,
    grows,
    mcol,
    xm,
    feat,
    pre,
    act,
    slope,
    flat,
    goals,
    masks,
    shuffle,
    halo,
    ex,
    hx,
    eg,
    hg,
    pmine,
    pall,
    sx,
    rx,
    sg,
    rg,
    sp,
    rp,
    rows_ref,
    x_ref,
    mask_ref,
    goal_ref,
    dw_ref,
    dwb_ref,
    gain_ref,
    lnb_ref,
    win_ref,
    bin_ref,
    wout_ref,
    bout_ref,
    ls_ref,
    wh_ref,
    loaded,
    *,
    slots,
    tile,
    size,
    nv,
):
    rim = size // 2
    half = tile // 2
    width = x_ref.shape[-1]
    lanes = width // 2
    cells = tile * tile
    group = width // tile
    depth = (size + 1) // 2
    wide = tile + 16
    me = lax.axis_index("tiles")
    mine = lax.axis_index("ens")
    west = lax.rem(me + columns - 1, columns)
    east = lax.rem(me + 1, columns)

    barrier = pltpu.get_barrier_semaphore()
    pl.semaphore_signal(barrier, inc=1, device_id={"tiles": west}, device_id_type=MESH)
    pl.semaphore_signal(barrier, inc=1, device_id={"tiles": east}, device_id_type=MESH)
    for p in range(1, members):
        pl.semaphore_signal(
            barrier, inc=1, device_id={"ens": lax.rem(mine + p, members)}, device_id_type=MESH
        )

    pairs = [(rows_hbm, rows_ref), (mask_hbm, mask_ref)]
    pairs += [(x_hbm.at[s], x_ref.at[s]) for s in range(slots)]
    pairs += [
        (dw_hbm, dw_ref),
        (goal_hbm, goal_ref),
        (wh_hbm, wh_ref),
        (ls_hbm, ls_ref),
        (wout_hbm, wout_ref),
        (bout_hbm, bout_ref),
        (dwb_hbm, dwb_ref),
        (gain_hbm, gain_ref),
        (lnb_hbm, lnb_ref),
        (win_hbm, win_ref),
        (bin_hbm, bin_ref),
    ]
    loads = [
        pltpu.make_async_copy(src, dst, loaded.at[n]) for n, (src, dst) in enumerate(pairs)
    ]
    for load in loads:
        load.start()

    zero_strip = jnp.zeros((rim, tile, width), bf16)
    for side in range(2):
        hx[side, slots] = zero_strip
        hg[side, slots] = zero_strip

    eye_tile = (
        lax.broadcasted_iota(jnp.int32, (tile, tile), 0)
        == lax.broadcasted_iota(jnp.int32, (tile, tile), 1)
    ).astype(f32)
    ones = jnp.ones((tile, width), bf16)

    def mask_slot(s, carry):
        live = (rows_ref[s, me] >= 0).astype(f32)
        m = mask_ref[s].astype(f32) * live
        spread = (m[:, None, :] * eye_tile[None]).reshape(cells, tile).astype(bf16)
        col = jnp.dot(spread, ones, preferred_element_type=f32)
        mcol[s] = col
        xv = x_ref[s].astype(f32).reshape(cells, width) * col
        xm[s] = xv.astype(bf16)
        edge = jnp.zeros((LEFT, width), f32)
        for y in range(tile):
            at = y * wide
            pad[s, at : at + LEFT, :] = edge
            pad[s, at + LEFT : at + LEFT + tile, :] = xv[y * tile : (y + 1) * tile]
            pad[s, at + LEFT + tile : at + wide, :] = edge
        return carry

    def relayout(s, carry):
        live = (rows_ref[s, me] >= 0).astype(f32)
        flat[nv * tile : (nv + 1) * tile, :tile] = mask_ref[s].astype(f32) * live
        flat[0 : nv * tile, :tile] = goal_ref[s].astype(f32).reshape(nv * tile, tile)
        lane = lax.broadcasted_iota(jnp.int32, (tile // group, width), 1)
        for v in range(nv + 1):
            total = None
            for r in range(group):
                piece = flat[pl.ds(v * tile + r, tile // group, stride=group), :]
                if r:
                    piece = pltpu.roll(piece, r * tile, 1)
                total = piece if r == 0 else jnp.where(lane >= r * tile, piece, total)
            if v < nv:
                goals[s, v] = total
            else:
                masks[s] = total
        return carry

    def strips(s, dst):
        for c in range(rim):
            at = pl.ds(LEFT + tile - rim + c, tile, stride=wide)
            dst[0, s, c] = pad[s, at, :].astype(bf16)
            at = pl.ds(LEFT + c, tile, stride=wide)
            dst[1, s, c] = pad[s, at, :].astype(bf16)

    for load in loads[: 2 + slots]:
        load.wait()
    lax.fori_loop(0, slots, mask_slot, 0)
    for s in range(slots):
        strips(s, ex)

    pl.semaphore_wait(barrier, 2 + members - 1)

    def edge_copy(src, dst, send, recv, side):
        return pltpu.make_async_remote_copy(
            src_ref=src,
            dst_ref=dst,
            send_sem=send,
            recv_sem=recv,
            device_id={"tiles": east if side == 0 else west},
            device_id_type=MESH,
        )

    x_copies = [
        edge_copy(ex.at[side], hx.at[side, pl.ds(0, slots)], sx.at[side], rx.at[side], side)
        for side in range(2)
    ]
    for copy in x_copies:
        copy.start()

    for load in loads[2 + slots :]:
        load.wait()

    low = lax.broadcasted_iota(jnp.int32, (8, width), 1) < lanes
    zero_row = jnp.zeros((1, width), f32)
    for part in range(2):
        taps[part, 0] = jnp.zeros((8, width), f32)
        taps[part, size + 1] = jnp.zeros((8, width), f32)
    for i in range(size):
        now = jnp.concatenate([dw_ref[i], zero_row], axis=0)
        before = jnp.concatenate([zero_row, dw_ref[i]], axis=0)
        taps[0, i + 1] = jnp.where(low, now, pltpu.roll(before, lanes, 1))
        taps[1, i + 1] = jnp.where(low, pltpu.roll(now, lanes, 1), before)

    diagonal = (
        lax.rem(lax.broadcasted_iota(jnp.int32, (lanes, width), 1), lanes)
        == lax.broadcasted_iota(jnp.int32, (lanes, width), 0)
    ).astype(f32).astype(bf16)

    def build_band(t, carry):
        part = t // (depth * depth)
        dy = lax.rem(t // depth, depth)
        dx = lax.rem(t, depth)
        for py in range(2):
            for px in range(2):
                for qy in range(2):
                    row = taps[part, 1 + 2 * dy + py - qy, pl.ds(2 * dx + px, 1), :]
                    row = jnp.broadcast_to(row, (16, width)).astype(bf16)
                    for u in range(0, lanes, 16):
                        at = (2 * py + px) * lanes + u
                        band[t, at : at + 16, qy * width : (qy + 1) * width] = (
                            row * diagonal[u : u + 16]
                        )
        return carry

    lax.fori_loop(0, 2 * depth * depth, build_band, 0)
    lax.fori_loop(0, slots, relayout, 0)

    scaled_head = wh_ref[...] * ls_ref[...]
    through_head = lax.dot_general(
        jnp.concatenate([scaled_head, scaled_head], axis=0), wout_ref[...].astype(f32), NT,
        precision=lax.Precision.HIGHEST, preferred_element_type=f32,
    )[:nv]
    bias_head = jnp.sum(scaled_head * bout_ref[...], axis=1, keepdims=True)
    both = jnp.concatenate([wh_ref[...], through_head], axis=1)
    both_hi = both.astype(bf16).astype(f32)
    both_hl = jnp.concatenate(
        [both_hi, both - both_hi, jnp.zeros((16 - 2 * nv, both.shape[1]), f32)], axis=0
    ).astype(bf16)

    half_lane = lax.broadcasted_iota(jnp.int32, (half, width), 1) < lanes

    def swap(first, second):
        lo = jnp.where(half_lane, first, pltpu.roll(second, lanes, 1))
        hi = jnp.where(half_lane, pltpu.roll(first, lanes, 1), second)
        return lo, hi

    def centre(flip):
        def one(s, carry):
            own = rows_ref[s, me]
            above = jnp.maximum(s - 1, 0)
            below = jnp.minimum(s + 1, slots - 1)
            flag_up = (
                (s > 0) & (own >= 0) & (rows_ref[above, me] == own - 1)
            ).astype(f32)
            flag_down = (
                (s < slots - 1) & (rows_ref[below, me] >= 0) & (rows_ref[below, me] == own + 1)
            ).astype(f32)
            for r in range(tile + 2 * rim):
                y = r - rim
                m, py = r // 2, r % 2
                for dx in range(depth):
                    found = []
                    for px in range(2):
                        at = pl.ds(
                            (y % tile) * wide + LEFT - rim + 2 * dx + px, half, stride=2
                        )
                        if y < 0:
                            piece = pad[above, at, :] * flag_up
                        elif y >= tile:
                            piece = pad[below, at, :] * flag_down
                        else:
                            piece = pad[s, at, :]
                        found.append(piece)
                    place = py
                    if flip:
                        found = found[::-1]
                        place = 1 - py
                    lo, hi = swap(*found)
                    lhs[0, dx, m, :, place * width : (place + 1) * width] = lo.astype(bf16)
                    lhs[1, dx, m, :, place * width : (place + 1) * width] = hi.astype(bf16)
            res = []
            for part in range(2):
                left = []
                right = []
                for dy in range(depth):
                    for dx in range(depth):
                        left.append(lhs[part, dx, dy : dy + half].reshape(half * half, 2 * width))
                        oy, ox = (depth - 1 - dy, depth - 1 - dx) if flip else (dy, dx)
                        right.append(band[(part * depth + oy) * depth + ox])
                res.append(
                    jnp.dot(
                        jnp.concatenate(left, axis=1),
                        jnp.concatenate(right, axis=0),
                        preferred_element_type=f32,
                    )
                )
            for qy in range(2):
                y = 1 - qy if flip else qy
                at = slice(qy * width, (qy + 1) * width)
                for k in range(half):
                    rows = slice(k * half, (k + 1) * half)
                    lo, hi = swap(res[0][rows, at], res[1][rows, at])
                    even, odd = (hi, lo) if flip else (lo, hi)
                    acc[s, pl.ds((2 * k + y) * tile, half, stride=2), :] = even
                    acc[s, pl.ds((2 * k + y) * tile + 1, half, stride=2), :] = odd
            return carry

        return one

    def edges(s, buf, flip):
        row = rows_ref[s, me]
        for side, source in ((0, west), (1, east)):
            there = [rows_ref[t, source] for t in range(slots)]

            def find(wanted):
                place = jnp.int32(slots)
                for t in range(slots):
                    place = jnp.where(
                        (there[t] >= 0) & (there[t] == wanted), jnp.int32(t), place
                    )
                return place

            up = find(row - 1)
            level = find(row)
            down = find(row + 1)
            total = [jnp.zeros((tile, width), f32) for _ in range(rim)]
            for c in range(rim):
                halo[side, c, 0:8] = buf[side, up, c].astype(f32)[tile - 8 :]
                halo[side, c, 8 : 8 + tile] = buf[side, level, c].astype(f32)
                halo[side, c, 8 + tile :] = buf[side, down, c].astype(f32)[:8]
                for dy in range(size):
                    piece = halo[side, c, 8 - rim + dy : 8 - rim + dy + tile]
                    for u in range(rim):
                        if (c < u) if side == 0 else (c > u):
                            continue
                        j = c - u if side == 0 else size - 1 + c - u
                        i, j = (size - 1 - dy, size - 1 - j) if flip else (dy, j)
                        total[u] = total[u] + dw_ref[i, j : j + 1, :] * piece
            for u in range(rim):
                col = u if side == 0 else tile - rim + u
                at = pl.ds(col, tile, stride=tile)
                acc[s, at, :] = acc[s, at, :] + total[u]

    def edges_all(buf, flip):
        def one(s, carry):
            edges(s, buf, flip)
            return carry

        lax.fori_loop(0, slots, one, 0)

    lax.fori_loop(0, slots, centre(False), 0)
    for copy in x_copies:
        copy.wait()
    edges_all(hx, False)

    strip_rows = 4
    chunk = strip_rows * tile
    small = 64
    nhalf = half * tile

    def pred_copy(s, p):
        return pltpu.make_async_remote_copy(
            src_ref=pmine.at[s],
            dst_ref=pall.at[p - 1, s],
            send_sem=sp.at[p - 1, s],
            recv_sem=rp.at[p - 1, s],
            device_id={"ens": lax.rem(mine + p, members)},
            device_id_type=MESH,
        )

    def forward(s, carry):
        for q in range(tile // strip_rows):
            at = slice(q * chunk, (q + 1) * chunk)
            z = acc[s, at, :] + dwb_ref[...]
            mean = jnp.mean(z, axis=1, keepdims=True)
            z = z - mean
            inv = lax.rsqrt(jnp.mean(z * z, axis=1, keepdims=True) + epsilon)
            z = z * inv
            normed[s, at, :] = z
            invs[s, at, :] = jnp.broadcast_to(inv, (chunk, width))
            feat[at, :] = (z * gain_ref[...] + lnb_ref[...]).astype(bf16)
        for b in range(2):
            base = b * nhalf
            pre[...] = jnp.dot(
                feat[base : base + nhalf, :], win_ref[...], preferred_element_type=f32
            )

            def gelu(q, carry):
                at = pl.ds(pl.multiple_of(q * small, small), small)
                v = pre[at, :] + bin_ref[...]
                cum = 0.5 * (1.0 + lax.erf(v * 0.7071067811865476))
                act[at, :] = (v * cum).astype(bf16)
                slope[s, b, at, :] = cum + v * jnp.exp(-0.5 * v * v) * 0.3989422804014327
                return carry

            lax.fori_loop(0, nhalf // small, gelu, 0, unroll=2)
            r16 = lax.dot_general(
                both_hl,
                jnp.concatenate([xm[s, base : base + nhalf, :], act[...]], axis=1),
                NT,
                preferred_element_type=f32,
            )
            r4 = r16[:nv] + r16[nv : 2 * nv] + bias_head
            for q in range(nhalf // width):
                pmine[s, pl.ds(b * (nhalf // width) + q, nv, stride=cells // width), :] = r4[
                    :, q * width : (q + 1) * width
                ]
        for p in range(1, members):
            pred_copy(s, p).start()
        return carry

    lax.fori_loop(0, slots, forward, 0)

    def gz_copy(s, side):
        return edge_copy(eg.at[side, s], hg.at[side, s], sg.at[side, s], rg.at[side, s], side)

    deep = cells // width

    def backward(s):
        for p in range(1, members):
            pred_copy(s, p).wait()
        every = [pmine[s].reshape(nv, deep, width)] + [
            pall[p - 1, s].reshape(nv, deep, width) for p in range(1, members)
        ]
        goal = goals[s]
        mask = masks[s]
        skill = soft_abs(every[0] - goal)
        spread = jnp.zeros_like(skill)
        pull = jnp.zeros_like(skill)
        for p in range(1, members):
            skill = skill + soft_abs(every[p] - goal)
            pull = pull + soft_sign(every[0] - every[p])
            for other in range(p):
                spread = spread + soft_abs(every[p] - every[other])
        same = members * softness**0.5
        score = mask * jnp.sum(
            skill / members - (2.0 * spread + same) / (2 * members * members), axis=0
        )
        for r in range(group):
            piece = pltpu.roll(score, width - r * tile, 1) if r else score
            shuffle[pl.ds(r, tile // group, stride=group), :] = piece
        share = tile // members
        piece = shuffle[pl.ds(pl.multiple_of(mine * share, share), share), :][:, :tile]
        crps_ref[s] = piece.astype(crps_ref.dtype)
        gp = mask[None] * (
            soft_sign(every[0] - goal) / members - pull / (members * members)
        )
        flat[0 : nv * deep, :] = gp.astype(bf16).astype(f32).reshape(nv * deep, width)
        for b in range(2):
            base = b * nhalf
            g4 = jnp.concatenate(
                [
                    flat[pl.ds(b * (nhalf // width) + q, nv, stride=deep), :]
                    for q in range(nhalf // width)
                ],
                axis=1,
            )
            gp16 = jnp.concatenate(
                [g4, g4, jnp.zeros((16 - 2 * nv, nhalf), f32)], axis=0
            ).astype(bf16)
            big = lax.dot_general(gp16, both_hl, TN, preferred_element_type=f32)
            grows[s, base : base + nhalf, :] = big[:, :width]
            act[...] = (big[:, width:] * slope[s, b]).astype(bf16)
            full = lax.dot_general(act[...], win_ref[...], NT, preferred_element_type=f32)
            for r in range(half):
                at = slice(base + r * tile, base + (r + 1) * tile)
                g = full[r * tile : (r + 1) * tile] * gain_ref[...]
                z = normed[s, at, :]
                g = invs[s, at, :] * (
                    g
                    - jnp.mean(g, axis=1, keepdims=True)
                    - z * jnp.mean(g * z, axis=1, keepdims=True)
                )
                at = (b * half + r) * wide + LEFT
                pad[s, at : at + tile, :] = g
        strips(s, eg)
        for side in range(2):
            gz_copy(s, side).start()

    def turn(t, carry):
        @pl.when(t < slots)
        def _():
            backward(t)

        @pl.when(t > 0)
        def _():
            centre(True)(t - 1, 0)

        return carry

    lax.fori_loop(0, slots + 1, turn, 0)
    for s in range(slots):
        for side in range(2):
            gz_copy(s, side).wait()

    def last(s, carry):
        edges(s, hg, True)
        v = mcol[s] * (grows[s] + acc[s])
        out_ref[s] = v.reshape(tile, tile, width).astype(bf16)
        return carry

    lax.fori_loop(0, slots, last, 0)


def on_device(
    inputs,
    slot_rows,
    cell_mask,
    target,
    dw_kernel,
    dw_bias,
    ln_gain,
    ln_bias,
    w_in,
    b_in,
    w_out,
    b_out,
    layer_scale,
    w_head,
):
    columns = lax.axis_size("tiles")
    members = lax.axis_size("ens")
    slots, tile, _, width = inputs.shape[3:]
    size = dw_kernel.shape[0]
    rim = size // 2
    half = tile // 2
    cells = tile * tile
    hidden = w_in.shape[1]
    nv = w_head.shape[1]
    vmem = pl.BlockSpec(memory_space=pltpu.VMEM)
    hbm = pl.BlockSpec(memory_space=pl.ANY)
    depth = (size + 1) // 2
    deep = cells // width
    strip = (2, slots, rim, tile, width)
    halo = (2, slots + 1, rim, tile, width)
    dma = pltpu.SemaphoreType.DMA
    operands = [
        slot_rows.T,
        inputs.reshape(slots, tile, tile, width),
        cell_mask.reshape(slots, tile, tile),
        target.reshape(slots, nv, tile, tile),
        dw_kernel,
        dw_bias[None],
        ln_gain[None],
        ln_bias[None],
        w_in,
        b_in[None],
        w_out,
        b_out[None],
        layer_scale[None],
        w_head.T,
    ]
    grad, score = pl.pallas_call(
        functools.partial(kernel, members, columns, slots=slots, tile=tile, size=size, nv=nv),
        out_shape=(
            pltpu.VMEM((slots, tile, tile, width), bf16),
            pltpu.VMEM((slots, tile // members, tile), bf16),
        ),
        in_specs=[hbm] * 14,
        out_specs=(vmem, vmem),
        scratch_shapes=[
            pltpu.VMEM((slots, tile * (tile + 16), width), f32),
            pltpu.VMEM((2, depth, half + rim, half, 2 * width), bf16),
            pltpu.VMEM((2, size + 2, 8, width), f32),
            pltpu.VMEM((2 * depth * depth, 2 * width, 2 * width), bf16),
            pltpu.VMEM((slots, cells, width), f32),
            pltpu.VMEM((slots, cells, width), f32),
            pltpu.VMEM((slots, cells, width), f32),
            pltpu.VMEM((slots, cells, width), f32),
            pltpu.VMEM((slots, cells, width), f32),
            pltpu.VMEM((slots, cells, width), bf16),
            pltpu.VMEM((cells, width), bf16),
            pltpu.VMEM((half * tile, hidden), f32),
            pltpu.VMEM((half * tile, hidden), bf16),
            pltpu.VMEM((slots, 2, half * tile, hidden), f32),
            pltpu.VMEM(((nv + 1) * tile, width), f32),
            pltpu.VMEM((slots, nv, deep, width), f32),
            pltpu.VMEM((slots, deep, width), f32),
            pltpu.VMEM((tile, width), f32),
            pltpu.VMEM((2, rim, tile + 16, width), f32),
            pltpu.VMEM(strip, bf16),
            pltpu.VMEM(halo, bf16),
            pltpu.VMEM(strip, bf16),
            pltpu.VMEM(halo, bf16),
            pltpu.VMEM((slots, nv * deep, width), f32),
            pltpu.VMEM((members - 1, slots, nv * deep, width), f32),
            dma((2,)),
            dma((2,)),
            dma((2, slots)),
            dma((2, slots)),
            dma((members - 1, slots)),
            dma((members - 1, slots)),
        ]
        + [
            (pltpu.SMEM if n == 0 else pltpu.VMEM)(a.shape, a.dtype)
            for n, a in enumerate(operands)
        ]
        + [dma((len(operands) + slots - 1,))],
        compiler_params=pltpu.CompilerParams(
            collective_id=0, has_side_effects=True, vmem_limit_bytes=60 * 2**20
        ),
    )(*[pltpu.with_memory_space_constraint(a, pltpu.HBM) for a in operands])
    return (grad.reshape(inputs.shape), score[None, None])


def solution(mesh):
    placed = (
        P("ens", "lev", ("groups", "tiles"), None, None, None, None),
        P("groups", None),
        P("lev", ("groups", "tiles"), None, None, None),
        P("lev", ("groups", "tiles"), None, None, None, None),
    ) + (P(),) * 10
    return jax.shard_map(
        on_device,
        mesh=mesh,
        in_specs=placed,
        out_specs=(
            P("ens", "lev", ("groups", "tiles"), None, None, None, None),
            P("lev", ("groups", "tiles"), None, "ens", None),
        ),
        check_vma=False,
    )
```

```python
import functools

import jax
import jax.numpy as jnp
from jax import lax
from jax.experimental import pallas as pl
from jax.experimental.pallas import tpu as pltpu
from jax.sharding import PartitionSpec as P

softness = 0.0625
epsilon = 1e-06
MESH = pl.DeviceIdType.MESH
f32 = jnp.float32
bf16 = jnp.bfloat16
LEFT = 8
NT = (((1,), (1,)), ((), ()))
TN = (((0,), (0,)), ((), ()))


def soft_abs(value):
    return jnp.sqrt(value * value + softness)


def soft_sign(value):
    return value * lax.rsqrt(value * value + softness)


def kernel(
    members,
    columns,
    rows_hbm,
    x_hbm,
    mask_hbm,
    goal_hbm,
    dw_hbm,
    dwb_hbm,
    gain_hbm,
    lnb_hbm,
    win_hbm,
    bin_hbm,
    wout_hbm,
    bout_hbm,
    ls_hbm,
    wh_hbm,
    out_ref,
    crps_ref,
    pad,
    lhs_lo,
    lhs_hi,
    taps,
    band,
    acc,
    normed,
    invs,
    grows,
    mcol,
    xm,
    feat,
    pre,
    act,
    slope,
    flat,
    goals,
    masks,
    shuffle,
    halo,
    ex,
    hx,
    eg,
    hg,
    pmine,
    pall,
    sx,
    rx,
    sg,
    rg,
    sp,
    rp,
    rows_ref,
    x_ref,
    mask_ref,
    goal_ref,
    dw_ref,
    dwb_ref,
    gain_ref,
    lnb_ref,
    win_ref,
    bin_ref,
    wout_ref,
    bout_ref,
    ls_ref,
    wh_ref,
    loaded,
    *,
    slots,
    tile,
    size,
    nv,
):
    rim = size // 2
    half = tile // 2
    width = x_ref.shape[-1]
    lanes = width // 2
    cells = tile * tile
    group = width // tile
    depth = (size + 1) // 2
    wide = tile + 16
    lhs = (lhs_lo, lhs_hi)
    me = lax.axis_index("tiles")
    mine = lax.axis_index("ens")
    west = lax.rem(me + columns - 1, columns)
    east = lax.rem(me + 1, columns)

    barrier = pltpu.get_barrier_semaphore()
    pl.semaphore_signal(barrier, inc=1, device_id={"tiles": west}, device_id_type=MESH)
    pl.semaphore_signal(barrier, inc=1, device_id={"tiles": east}, device_id_type=MESH)
    for p in range(1, members):
        pl.semaphore_signal(
            barrier, inc=1, device_id={"ens": lax.rem(mine + p, members)}, device_id_type=MESH
        )

    pairs = [(rows_hbm, rows_ref), (mask_hbm, mask_ref)]
    pairs += [(x_hbm.at[s], x_ref.at[s]) for s in range(slots)]
    pairs += [
        (dw_hbm, dw_ref),
        (goal_hbm, goal_ref),
        (wh_hbm, wh_ref),
        (ls_hbm, ls_ref),
        (wout_hbm, wout_ref),
        (bout_hbm, bout_ref),
        (dwb_hbm, dwb_ref),
        (gain_hbm, gain_ref),
        (lnb_hbm, lnb_ref),
        (win_hbm, win_ref),
        (bin_hbm, bin_ref),
    ]
    loads = [
        pltpu.make_async_copy(src, dst, loaded.at[n]) for n, (src, dst) in enumerate(pairs)
    ]
    for load in loads:
        load.start()

    zero_strip = jnp.zeros((rim, tile, width), bf16)
    for side in range(2):
        hx[side, slots] = zero_strip
        hg[side, slots] = zero_strip

    eye_tile = (
        lax.broadcasted_iota(jnp.int32, (tile, tile), 0)
        == lax.broadcasted_iota(jnp.int32, (tile, tile), 1)
    ).astype(f32)
    ones = jnp.ones((tile, width), bf16)

    def mask_slot(s, carry):
        live = (rows_ref[s, me] >= 0).astype(f32)
        m = mask_ref[s].astype(f32) * live
        spread = (m[:, None, :] * eye_tile[None]).reshape(cells, tile).astype(bf16)
        col = jnp.dot(spread, ones, preferred_element_type=f32)
        mcol[s] = col
        xv = x_ref[s].astype(f32).reshape(cells, width) * col
        xm[s] = xv.astype(bf16)
        edge = jnp.zeros((LEFT, width), f32)
        for y in range(tile):
            at = y * wide
            pad[s, at : at + LEFT, :] = edge
            pad[s, at + LEFT : at + LEFT + tile, :] = xv[y * tile : (y + 1) * tile]
            pad[s, at + LEFT + tile : at + wide, :] = edge
        return carry

    def relayout(s, carry):
        live = (rows_ref[s, me] >= 0).astype(f32)
        flat[nv * tile : (nv + 1) * tile, :tile] = mask_ref[s].astype(f32) * live
        flat[0 : nv * tile, :tile] = goal_ref[s].astype(f32).reshape(nv * tile, tile)
        lane = lax.broadcasted_iota(jnp.int32, (tile // group, width), 1)
        for v in range(nv + 1):
            total = None
            for r in range(group):
                piece = flat[pl.ds(v * tile + r, tile // group, stride=group), :]
                if r:
                    piece = pltpu.roll(piece, r * tile, 1)
                total = piece if r == 0 else jnp.where(lane >= r * tile, piece, total)
            if v < nv:
                goals[s, v] = total
            else:
                masks[s] = total
        return carry

    def strips(s, dst):
        for c in range(rim):
            at = pl.ds(LEFT + tile - rim + c, tile, stride=wide)
            dst[0, s, c] = pad[s, at, :].astype(bf16)
            at = pl.ds(LEFT + c, tile, stride=wide)
            dst[1, s, c] = pad[s, at, :].astype(bf16)

    for load in loads[: 2 + slots]:
        load.wait()
    lax.fori_loop(0, slots, mask_slot, 0)
    for s in range(slots):
        strips(s, ex)

    pl.semaphore_wait(barrier, 2 + members - 1)

    def edge_copy(src, dst, send, recv, side):
        return pltpu.make_async_remote_copy(
            src_ref=src,
            dst_ref=dst,
            send_sem=send,
            recv_sem=recv,
            device_id={"tiles": east if side == 0 else west},
            device_id_type=MESH,
        )

    x_copies = [
        edge_copy(ex.at[side], hx.at[side, pl.ds(0, slots)], sx.at[side], rx.at[side], side)
        for side in range(2)
    ]
    for copy in x_copies:
        copy.start()

    for load in loads[2 + slots :]:
        load.wait()

    low = lax.broadcasted_iota(jnp.int32, (8, width), 1) < lanes
    zero_row = jnp.zeros((1, width), f32)
    for part in range(2):
        taps[part, 0] = jnp.zeros((8, width), f32)
        taps[part, size + 1] = jnp.zeros((8, width), f32)
    for i in range(size):
        now = jnp.concatenate([dw_ref[i], zero_row], axis=0)
        before = jnp.concatenate([zero_row, dw_ref[i]], axis=0)
        taps[0, i + 1] = jnp.where(low, now, pltpu.roll(before, lanes, 1))
        taps[1, i + 1] = jnp.where(low, pltpu.roll(now, lanes, 1), before)

    diagonal = (
        lax.rem(lax.broadcasted_iota(jnp.int32, (lanes, width), 1), lanes)
        == lax.broadcasted_iota(jnp.int32, (lanes, width), 0)
    ).astype(f32).astype(bf16)

    def build_band(t, carry):
        part = t // (depth * depth)
        dy = lax.rem(t // depth, depth)
        dx = lax.rem(t, depth)
        for py in range(2):
            for px in range(2):
                for qy in range(2):
                    row = taps[part, 1 + 2 * dy + py - qy, pl.ds(2 * dx + px, 1), :]
                    row = jnp.broadcast_to(row, (16, width)).astype(bf16)
                    for u in range(0, lanes, 16):
                        at = (2 * py + px) * lanes + u
                        band[t, at : at + 16, qy * width : (qy + 1) * width] = (
                            row * diagonal[u : u + 16]
                        )
        return carry

    lax.fori_loop(0, 2 * depth * depth, build_band, 0, unroll=4)
    lax.fori_loop(0, slots, relayout, 0)

    scaled_head = wh_ref[...] * ls_ref[...]
    through_head = lax.dot_general(
        jnp.concatenate([scaled_head, scaled_head], axis=0), wout_ref[...].astype(f32), NT,
        precision=lax.Precision.HIGHEST, preferred_element_type=f32,
    )[:nv]
    bias_head = jnp.sum(scaled_head * bout_ref[...], axis=1, keepdims=True)
    both = jnp.concatenate([wh_ref[...], through_head], axis=1)
    both_hi = both.astype(bf16).astype(f32)
    both_hl = jnp.concatenate(
        [both_hi, both - both_hi, jnp.zeros((16 - 2 * nv, both.shape[1]), f32)], axis=0
    ).astype(bf16)

    half_lane = lax.broadcasted_iota(jnp.int32, (half, width), 1) < lanes

    def swap(first, second):
        lo = jnp.where(half_lane, first, pltpu.roll(second, lanes, 1))
        hi = jnp.where(half_lane, pltpu.roll(first, lanes, 1), second)
        return lo, hi

    def centre(flip):
        own = [rows_ref[s, me] for s in range(slots)]
        res = []
        for part in range(2):
            for s in range(slots):
                above, below = max(s - 1, 0), min(s + 1, slots - 1)
                flag_up = ((s > 0) & (own[s] >= 0) & (own[above] == own[s] - 1)).astype(f32)
                flag_down = (
                    (s < slots - 1) & (own[below] >= 0) & (own[below] == own[s] + 1)
                ).astype(f32)
                for r in range(tile + 2 * rim):
                    y = r - rim
                    m, py = r // 2, r % 2
                    for dx in range(depth):
                        found = []
                        for px in range(2):
                            at = pl.ds(
                                (y % tile) * wide + LEFT - rim + 2 * dx + px, half, stride=2
                            )
                            if y < 0:
                                piece = pad[above, at, :] * flag_up
                            elif y >= tile:
                                piece = pad[below, at, :] * flag_down
                            else:
                                piece = pad[s, at, :]
                            found.append(piece.astype(bf16))
                        place = py
                        if flip:
                            found = found[::-1]
                            place = 1 - py
                        cut = slice(part * lanes, (part + 1) * lanes)
                        lhs[part][s, dx, m, :, place * width : (place + 1) * width] = (
                            jnp.concatenate([found[0][:, cut], found[1][:, cut]], axis=1)
                        )
            left = []
            right = []
            for dy in range(depth):
                for dx in range(depth):
                    left.append(
                        lhs[part][:, dx, dy : dy + half].reshape(
                            slots * half * half, 2 * width
                        )
                    )
                    oy, ox = (depth - 1 - dy, depth - 1 - dx) if flip else (dy, dx)
                    right.append(band[(part * depth + oy) * depth + ox])
            res.append(
                jnp.dot(
                    jnp.concatenate(left, axis=1),
                    jnp.concatenate(right, axis=0),
                    preferred_element_type=f32,
                )
            )
        for s in range(slots):
            for qy in range(2):
                y = 1 - qy if flip else qy
                at = slice(qy * width, (qy + 1) * width)
                for k in range(half):
                    base = (s * half + k) * half
                    rows = slice(base, base + half)
                    lo, hi = swap(res[0][rows, at], res[1][rows, at])
                    even, odd = (hi, lo) if flip else (lo, hi)
                    acc[s, pl.ds((2 * k + y) * tile, half, stride=2), :] = even
                    acc[s, pl.ds((2 * k + y) * tile + 1, half, stride=2), :] = odd

    def edges(s, buf, flip):
        row = rows_ref[s, me]
        for side, source in ((0, west), (1, east)):
            there = [rows_ref[t, source] for t in range(slots)]

            def find(wanted):
                place = jnp.int32(slots)
                for t in range(slots):
                    place = jnp.where(
                        (there[t] >= 0) & (there[t] == wanted), jnp.int32(t), place
                    )
                return place

            up = find(row - 1)
            level = find(row)
            down = find(row + 1)
            total = [jnp.zeros((tile, width), f32) for _ in range(rim)]
            for c in range(rim):
                halo[side, c, 0:8] = buf[side, up, c].astype(f32)[tile - 8 :]
                halo[side, c, 8 : 8 + tile] = buf[side, level, c].astype(f32)
                halo[side, c, 8 + tile :] = buf[side, down, c].astype(f32)[:8]
                for dy in range(size):
                    piece = halo[side, c, 8 - rim + dy : 8 - rim + dy + tile]
                    for u in range(rim):
                        if (c < u) if side == 0 else (c > u):
                            continue
                        j = c - u if side == 0 else size - 1 + c - u
                        i, j = (size - 1 - dy, size - 1 - j) if flip else (dy, j)
                        total[u] = total[u] + dw_ref[i, j : j + 1, :] * piece
            for u in range(rim):
                col = u if side == 0 else tile - rim + u
                at = pl.ds(col, tile, stride=tile)
                acc[s, at, :] = acc[s, at, :] + total[u]

    def edges_all(buf, flip):
        def one(s, carry):
            edges(s, buf, flip)
            return carry

        lax.fori_loop(0, slots, one, 0)

    centre(False)
    for copy in x_copies:
        copy.wait()
    edges_all(hx, False)

    strip_rows = 4
    chunk = strip_rows * tile
    small = 64
    nhalf = half * tile

    def pred_copy(s, p):
        return pltpu.make_async_remote_copy(
            src_ref=pmine.at[s],
            dst_ref=pall.at[p - 1, s],
            send_sem=sp.at[p - 1, s],
            recv_sem=rp.at[p - 1, s],
            device_id={"ens": lax.rem(mine + p, members)},
            device_id_type=MESH,
        )

    def forward(s, carry):
        for q in range(tile // strip_rows):
            at = slice(q * chunk, (q + 1) * chunk)
            z = acc[s, at, :] + dwb_ref[...]
            mean = jnp.mean(z, axis=1, keepdims=True)
            z = z - mean
            inv = lax.rsqrt(jnp.mean(z * z, axis=1, keepdims=True) + epsilon)
            z = z * inv
            normed[s, at, :] = z
            invs[s, at, :] = jnp.broadcast_to(inv, (chunk, width))
            feat[at, :] = (z * gain_ref[...] + lnb_ref[...]).astype(bf16)
        for b in range(2):
            base = b * nhalf
            pre[b] = jnp.dot(
                feat[base : base + nhalf, :], win_ref[...], preferred_element_type=f32
            )

            for q in range(nhalf // small):
                at = slice(q * small, (q + 1) * small)
                v = pre[b, at, :] + bin_ref[...]
                cum = 0.5 * (1.0 + lax.erf(v * 0.7071067811865476))
                act[b, at, :] = (v * cum).astype(bf16)
                slope[s, b, at, :] = cum + v * jnp.exp(-0.5 * v * v) * 0.3989422804014327
            r16 = lax.dot_general(
                both_hl,
                jnp.concatenate([xm[s, base : base + nhalf, :], act[b]], axis=1),
                NT,
                preferred_element_type=f32,
            )
            r4 = r16[:nv] + r16[nv : 2 * nv] + bias_head
            for q in range(nhalf // width):
                pmine[s, pl.ds(b * (nhalf // width) + q, nv, stride=cells // width), :] = r4[
                    :, q * width : (q + 1) * width
                ]
        for p in range(1, members):
            pred_copy(s, p).start()
        return carry

    lax.fori_loop(0, slots, forward, 0)

    def gz_copy(s, side):
        return edge_copy(eg.at[side, s], hg.at[side, s], sg.at[side, s], rg.at[side, s], side)

    deep = cells // width

    def backward(s, carry):
        for p in range(1, members):
            pred_copy(s, p).wait()
        every = [pmine[s].reshape(nv, deep, width)] + [
            pall[p - 1, s].reshape(nv, deep, width) for p in range(1, members)
        ]
        goal = goals[s]
        mask = masks[s]
        skill = soft_abs(every[0] - goal)
        spread = jnp.zeros_like(skill)
        pull = jnp.zeros_like(skill)
        for p in range(1, members):
            skill = skill + soft_abs(every[p] - goal)
            pull = pull + soft_sign(every[0] - every[p])
            for other in range(p):
                spread = spread + soft_abs(every[p] - every[other])
        same = members * softness**0.5
        score = mask * jnp.sum(
            skill / members - (2.0 * spread + same) / (2 * members * members), axis=0
        )
        for r in range(group):
            piece = pltpu.roll(score, width - r * tile, 1) if r else score
            shuffle[pl.ds(r, tile // group, stride=group), :] = piece
        share = tile // members
        piece = shuffle[pl.ds(pl.multiple_of(mine * share, share), share), :][:, :tile]
        crps_ref[s] = piece.astype(crps_ref.dtype)
        gp = mask[None] * (
            soft_sign(every[0] - goal) / members - pull / (members * members)
        )
        flat[0 : nv * deep, :] = gp.astype(bf16).astype(f32).reshape(nv * deep, width)
        for b in range(2):
            base = b * nhalf
            g4 = jnp.concatenate(
                [
                    flat[pl.ds(b * (nhalf // width) + q, nv, stride=deep), :]
                    for q in range(nhalf // width)
                ],
                axis=1,
            )
            gp16 = jnp.concatenate(
                [g4, g4, jnp.zeros((16 - 2 * nv, nhalf), f32)], axis=0
            ).astype(bf16)
            big = lax.dot_general(gp16, both_hl, TN, preferred_element_type=f32)
            grows[s, base : base + nhalf, :] = big[:, :width]
            act[b] = (big[:, width:] * slope[s, b]).astype(bf16)
            full = lax.dot_general(act[b], win_ref[...], NT, preferred_element_type=f32)
            for r in range(half):
                at = slice(base + r * tile, base + (r + 1) * tile)
                g = full[r * tile : (r + 1) * tile] * gain_ref[...]
                z = normed[s, at, :]
                g = invs[s, at, :] * (
                    g
                    - jnp.mean(g, axis=1, keepdims=True)
                    - z * jnp.mean(g * z, axis=1, keepdims=True)
                )
                at = (b * half + r) * wide + LEFT
                pad[s, at : at + tile, :] = g
        strips(s, eg)
        for side in range(2):
            gz_copy(s, side).start()

        return carry

    lax.fori_loop(0, slots, backward, 0)
    centre(True)
    for s in range(slots):
        for side in range(2):
            gz_copy(s, side).wait()

    def last(s, carry):
        edges(s, hg, True)
        v = mcol[s] * (grows[s] + acc[s])
        out_ref[s] = v.reshape(tile, tile, width).astype(bf16)
        return carry

    lax.fori_loop(0, slots, last, 0)


def on_device(
    inputs,
    slot_rows,
    cell_mask,
    target,
    dw_kernel,
    dw_bias,
    ln_gain,
    ln_bias,
    w_in,
    b_in,
    w_out,
    b_out,
    layer_scale,
    w_head,
):
    columns = lax.axis_size("tiles")
    members = lax.axis_size("ens")
    slots, tile, _, width = inputs.shape[3:]
    size = dw_kernel.shape[0]
    rim = size // 2
    half = tile // 2
    cells = tile * tile
    hidden = w_in.shape[1]
    nv = w_head.shape[1]
    vmem = pl.BlockSpec(memory_space=pltpu.VMEM)
    hbm = pl.BlockSpec(memory_space=pl.ANY)
    depth = (size + 1) // 2
    deep = cells // width
    strip = (2, slots, rim, tile, width)
    halo = (2, slots + 1, rim, tile, width)
    dma = pltpu.SemaphoreType.DMA
    operands = [
        slot_rows.T,
        inputs.reshape(slots, tile, tile, width),
        cell_mask.reshape(slots, tile, tile),
        target.reshape(slots, nv, tile, tile),
        dw_kernel,
        dw_bias[None],
        ln_gain[None],
        ln_bias[None],
        w_in,
        b_in[None],
        w_out,
        b_out[None],
        layer_scale[None],
        w_head.T,
    ]
    grad, score = pl.pallas_call(
        functools.partial(kernel, members, columns, slots=slots, tile=tile, size=size, nv=nv),
        out_shape=(
            pltpu.VMEM((slots, tile, tile, width), bf16),
            pltpu.VMEM((slots, tile // members, tile), bf16),
        ),
        in_specs=[hbm] * 14,
        out_specs=(vmem, vmem),
        scratch_shapes=[
            pltpu.VMEM((slots, tile * (tile + 16), width), f32),
            pltpu.VMEM((slots, depth, half + rim, half, 2 * width), bf16),
            pltpu.VMEM((slots, depth, half + rim, half, 2 * width), bf16),
            pltpu.VMEM((2, size + 2, 8, width), f32),
            pltpu.VMEM((2 * depth * depth, 2 * width, 2 * width), bf16),
            pltpu.VMEM((slots, cells, width), f32),
            pltpu.VMEM((slots, cells, width), f32),
            pltpu.VMEM((slots, cells, width), f32),
            pltpu.VMEM((slots, cells, width), f32),
            pltpu.VMEM((slots, cells, width), f32),
            pltpu.VMEM((slots, cells, width), bf16),
            pltpu.VMEM((cells, width), bf16),
            pltpu.VMEM((2, half * tile, hidden), f32),
            pltpu.VMEM((2, half * tile, hidden), bf16),
            pltpu.VMEM((slots, 2, half * tile, hidden), f32),
            pltpu.VMEM(((nv + 1) * tile, width), f32),
            pltpu.VMEM((slots, nv, deep, width), f32),
            pltpu.VMEM((slots, deep, width), f32),
            pltpu.VMEM((tile, width), f32),
            pltpu.VMEM((2, rim, tile + 16, width), f32),
            pltpu.VMEM(strip, bf16),
            pltpu.VMEM(halo, bf16),
            pltpu.VMEM(strip, bf16),
            pltpu.VMEM(halo, bf16),
            pltpu.VMEM((slots, nv * deep, width), f32),
            pltpu.VMEM((members - 1, slots, nv * deep, width), f32),
            dma((2,)),
            dma((2,)),
            dma((2, slots)),
            dma((2, slots)),
            dma((members - 1, slots)),
            dma((members - 1, slots)),
        ]
        + [
            (pltpu.SMEM if n == 0 else pltpu.VMEM)(a.shape, a.dtype)
            for n, a in enumerate(operands)
        ]
        + [dma((len(operands) + slots - 1,))],
        compiler_params=pltpu.CompilerParams(
            collective_id=0, has_side_effects=True, vmem_limit_bytes=60 * 2**20
        ),
    )(*[pltpu.with_memory_space_constraint(a, pltpu.HBM) for a in operands])
    return (grad.reshape(inputs.shape), score[None, None])


def solution(mesh):
    placed = (
        P("ens", "lev", ("groups", "tiles"), None, None, None, None),
        P("groups", None),
        P("lev", ("groups", "tiles"), None, None, None),
        P("lev", ("groups", "tiles"), None, None, None, None),
    ) + (P(),) * 10
    return jax.shard_map(
        on_device,
        mesh=mesh,
        in_specs=placed,
        out_specs=(
            P("ens", "lev", ("groups", "tiles"), None, None, None, None),
            P("lev", ("groups", "tiles"), None, "ens", None),
        ),
        check_vma=False,
    )
```

```python
import functools

import jax
import jax.numpy as jnp
from jax import lax
from jax.experimental import pallas as pl
from jax.experimental.pallas import tpu as pltpu
from jax.sharding import PartitionSpec as P

softness = 0.0625
epsilon = 1e-06
MESH = pl.DeviceIdType.MESH
f32 = jnp.float32
bf16 = jnp.bfloat16
LEFT = 8
NT = (((1,), (1,)), ((), ()))
TN = (((0,), (0,)), ((), ()))


def soft_abs(value):
    return jnp.sqrt(value * value + softness)


def soft_sign(value):
    return value * lax.rsqrt(value * value + softness)


def kernel(
    members,
    columns,
    rows_hbm,
    x_hbm,
    mask_hbm,
    goal_hbm,
    dw_hbm,
    dwb_hbm,
    gain_hbm,
    lnb_hbm,
    win_hbm,
    bin_hbm,
    wout_hbm,
    bout_hbm,
    ls_hbm,
    wh_hbm,
    out_ref,
    crps_ref,
    pad,
    lhs_lo,
    lhs_hi,
    taps,
    band_lo,
    band_hi,
    acc,
    normed,
    invs,
    grows,
    mcol,
    xm,
    feat,
    pre,
    act,
    slope,
    flat,
    goals,
    masks,
    shuffle,
    halo,
    ex,
    hx,
    eg,
    hg,
    pmine,
    pall,
    sx,
    rx,
    sg,
    rg,
    sp,
    rp,
    rows_ref,
    x_ref,
    mask_ref,
    goal_ref,
    dw_ref,
    dwb_ref,
    gain_ref,
    lnb_ref,
    win_ref,
    bin_ref,
    wout_ref,
    bout_ref,
    ls_ref,
    wh_ref,
    loaded,
    *,
    slots,
    tile,
    size,
    nv,
):
    rim = size // 2
    half = tile // 2
    width = x_ref.shape[-1]
    lanes = width // 2
    cells = tile * tile
    group = width // tile
    depth = (size + 1) // 2
    wide = tile + 16
    lhs = (lhs_lo, lhs_hi)
    band = (band_lo, band_hi)
    me = lax.axis_index("tiles")
    mine = lax.axis_index("ens")
    west = lax.rem(me + columns - 1, columns)
    east = lax.rem(me + 1, columns)

    barrier = pltpu.get_barrier_semaphore()
    pl.semaphore_signal(barrier, inc=1, device_id={"tiles": west}, device_id_type=MESH)
    pl.semaphore_signal(barrier, inc=1, device_id={"tiles": east}, device_id_type=MESH)
    for p in range(1, members):
        pl.semaphore_signal(
            barrier, inc=1, device_id={"ens": lax.rem(mine + p, members)}, device_id_type=MESH
        )

    pairs = [(dw_hbm, dw_ref), (rows_hbm, rows_ref), (mask_hbm, mask_ref)]
    pairs += [(x_hbm.at[s], x_ref.at[s]) for s in range(slots)]
    pairs += [
        (goal_hbm, goal_ref),
        (wh_hbm, wh_ref),
        (ls_hbm, ls_ref),
        (wout_hbm, wout_ref),
        (bout_hbm, bout_ref),
        (dwb_hbm, dwb_ref),
        (gain_hbm, gain_ref),
        (lnb_hbm, lnb_ref),
        (win_hbm, win_ref),
        (bin_hbm, bin_ref),
    ]
    loads = [
        pltpu.make_async_copy(src, dst, loaded.at[n]) for n, (src, dst) in enumerate(pairs)
    ]
    for load in loads:
        load.start()

    zero_strip = jnp.zeros((rim, tile, width), bf16)
    for side in range(2):
        hx[side, slots] = zero_strip
        hg[side, slots] = zero_strip

    eye_tile = (
        lax.broadcasted_iota(jnp.int32, (tile, tile), 0)
        == lax.broadcasted_iota(jnp.int32, (tile, tile), 1)
    ).astype(f32)
    ones = jnp.ones((tile, width), bf16)

    def mask_slot(s, carry):
        live = (rows_ref[s, me] >= 0).astype(f32)
        m = mask_ref[s].astype(f32) * live
        spread = (m[:, None, :] * eye_tile[None]).reshape(cells, tile).astype(bf16)
        col = jnp.dot(spread, ones, preferred_element_type=f32)
        mcol[s] = col
        xv = x_ref[s].astype(f32).reshape(cells, width) * col
        xm[s] = xv.astype(bf16)
        edge = jnp.zeros((LEFT, width), f32)
        for y in range(tile):
            at = y * wide
            pad[s, at : at + LEFT, :] = edge
            pad[s, at + LEFT : at + LEFT + tile, :] = xv[y * tile : (y + 1) * tile]
            pad[s, at + LEFT + tile : at + wide, :] = edge
        return carry

    def relayout(s):
        live = (rows_ref[s, me] >= 0).astype(f32)
        flat[s, nv * tile : (nv + 1) * tile, :tile] = mask_ref[s].astype(f32) * live
        flat[s, 0 : nv * tile, :tile] = goal_ref[s].astype(f32).reshape(nv * tile, tile)
        lane = lax.broadcasted_iota(jnp.int32, (tile // group, width), 1)
        for v in range(nv + 1):
            total = None
            for r in range(group):
                piece = flat[s, pl.ds(v * tile + r, tile // group, stride=group), :]
                if r:
                    piece = pltpu.roll(piece, r * tile, 1)
                total = piece if r == 0 else jnp.where(lane >= r * tile, piece, total)
            if v < nv:
                goals[s, v] = total
            else:
                masks[s] = total

    def strips(s, dst):
        for c in range(rim):
            at = pl.ds(LEFT + tile - rim + c, tile, stride=wide)
            dst[0, s, c] = pad[s, at, :].astype(bf16)
            at = pl.ds(LEFT + c, tile, stride=wide)
            dst[1, s, c] = pad[s, at, :].astype(bf16)

    loads[0].wait()
    low = lax.broadcasted_iota(jnp.int32, (8, width), 1) < lanes
    zero_row = jnp.zeros((1, width), f32)
    for part in range(2):
        taps[part, 0] = jnp.zeros((8, width), f32)
        taps[part, size + 1] = jnp.zeros((8, width), f32)
    for i in range(size):
        now = jnp.concatenate([dw_ref[i], zero_row], axis=0)
        before = jnp.concatenate([zero_row, dw_ref[i]], axis=0)
        taps[0, i + 1] = jnp.where(low, now, pltpu.roll(before, lanes, 1))
        taps[1, i + 1] = jnp.where(low, pltpu.roll(now, lanes, 1), before)

    diagonal = (
        lax.rem(lax.broadcasted_iota(jnp.int32, (lanes, width), 1), lanes)
        == lax.broadcasted_iota(jnp.int32, (lanes, width), 0)
    ).astype(f32).astype(bf16)

    def build_band(part, t):
        dy, dx = t // depth, lax.rem(t, depth)
        for py in range(2):
            for px in range(2):
                for qy in range(2):
                    row = taps[part, 1 + 2 * dy + py - qy, pl.ds(2 * dx + px, 1), :]
                    row = jnp.broadcast_to(row, (16, width)).astype(bf16)
                    for u in range(0, lanes, 16):
                        at = (2 * py + px) * lanes + u
                        band[part][t, at : at + 16, qy * width : (qy + 1) * width] = (
                            row * diagonal[u : u + 16]
                        )

    def build_low(t, carry):
        build_band(0, t)
        return carry

    lax.fori_loop(0, depth * depth, build_low, 0, unroll=4)

    for load in loads[1 : 3 + slots]:
        load.wait()
    lax.fori_loop(0, slots, mask_slot, 0)
    for s in range(slots):
        strips(s, ex)

    pl.semaphore_wait(barrier, 2 + members - 1)

    def edge_copy(src, dst, send, recv, side):
        return pltpu.make_async_remote_copy(
            src_ref=src,
            dst_ref=dst,
            send_sem=send,
            recv_sem=recv,
            device_id={"tiles": east if side == 0 else west},
            device_id_type=MESH,
        )

    x_copies = [
        edge_copy(ex.at[side], hx.at[side, pl.ds(0, slots)], sx.at[side], rx.at[side], side)
        for side in range(2)
    ]
    for copy in x_copies:
        copy.start()

    for load in loads[3 + slots :]:
        load.wait()

    scaled_head = wh_ref[...] * ls_ref[...]
    through_head = lax.dot_general(
        jnp.concatenate([scaled_head, scaled_head], axis=0), wout_ref[...].astype(f32), NT,
        precision=lax.Precision.HIGHEST, preferred_element_type=f32,
    )[:nv]
    bias_head = jnp.sum(scaled_head * bout_ref[...], axis=1, keepdims=True)
    both = jnp.concatenate([wh_ref[...], through_head], axis=1)
    both_hi = both.astype(bf16).astype(f32)
    both_hl = jnp.concatenate(
        [both_hi, both - both_hi, jnp.zeros((16 - 2 * nv, both.shape[1]), f32)], axis=0
    ).astype(bf16)

    half_lane = lax.broadcasted_iota(jnp.int32, (half, width), 1) < lanes

    def swap(first, second):
        lo = jnp.where(half_lane, first, pltpu.roll(second, lanes, 1))
        hi = jnp.where(half_lane, pltpu.roll(first, lanes, 1), second)
        return lo, hi

    def centre(flip, beside):
        own = [rows_ref[s, me] for s in range(slots)]
        res = []
        for part in range(2):
            if part == 1:
                beside()
            for s in range(slots):
                above, below = max(s - 1, 0), min(s + 1, slots - 1)
                flag_up = ((s > 0) & (own[s] >= 0) & (own[above] == own[s] - 1)).astype(f32)
                flag_down = (
                    (s < slots - 1) & (own[below] >= 0) & (own[below] == own[s] + 1)
                ).astype(f32)
                for r in range(tile + 2 * rim):
                    y = r - rim
                    m, py = r // 2, r % 2
                    for dx in range(depth):
                        found = []
                        for px in range(2):
                            at = pl.ds(
                                (y % tile) * wide + LEFT - rim + 2 * dx + px, half, stride=2
                            )
                            if y < 0:
                                piece = pad[above, at, :] * flag_up
                            elif y >= tile:
                                piece = pad[below, at, :] * flag_down
                            else:
                                piece = pad[s, at, :]
                            found.append(piece.astype(bf16))
                        place = py
                        if flip:
                            found = found[::-1]
                            place = 1 - py
                        cut = slice(part * lanes, (part + 1) * lanes)
                        lhs[part][s, dx, m, :, place * width : (place + 1) * width] = (
                            jnp.concatenate([found[0][:, cut], found[1][:, cut]], axis=1)
                        )
            left = []
            right = []
            for dy in range(depth):
                for dx in range(depth):
                    left.append(
                        lhs[part][:, dx, dy : dy + half].reshape(
                            slots * half * half, 2 * width
                        )
                    )
                    oy, ox = (depth - 1 - dy, depth - 1 - dx) if flip else (dy, dx)
                    right.append(band[part][oy * depth + ox])
            res.append(
                jnp.dot(
                    jnp.concatenate(left, axis=1),
                    jnp.concatenate(right, axis=0),
                    preferred_element_type=f32,
                )
            )
        for s in range(slots):
            for qy in range(2):
                y = 1 - qy if flip else qy
                at = slice(qy * width, (qy + 1) * width)
                for k in range(half):
                    base = (s * half + k) * half
                    rows = slice(base, base + half)
                    lo, hi = swap(res[0][rows, at], res[1][rows, at])
                    even, odd = (hi, lo) if flip else (lo, hi)
                    acc[s, pl.ds((2 * k + y) * tile, half, stride=2), :] = even
                    acc[s, pl.ds((2 * k + y) * tile + 1, half, stride=2), :] = odd

    def edges(s, buf, flip):
        row = rows_ref[s, me]
        for side, source in ((0, west), (1, east)):
            there = [rows_ref[t, source] for t in range(slots)]

            def find(wanted):
                place = jnp.int32(slots)
                for t in range(slots):
                    place = jnp.where(
                        (there[t] >= 0) & (there[t] == wanted), jnp.int32(t), place
                    )
                return place

            up = find(row - 1)
            level = find(row)
            down = find(row + 1)
            total = [jnp.zeros((tile, width), f32) for _ in range(rim)]
            for c in range(rim):
                halo[side, c, 0:8] = buf[side, up, c].astype(f32)[tile - 8 :]
                halo[side, c, 8 : 8 + tile] = buf[side, level, c].astype(f32)
                halo[side, c, 8 + tile :] = buf[side, down, c].astype(f32)[:8]
                for dy in range(size):
                    piece = halo[side, c, 8 - rim + dy : 8 - rim + dy + tile]
                    for u in range(rim):
                        if (c < u) if side == 0 else (c > u):
                            continue
                        j = c - u if side == 0 else size - 1 + c - u
                        i, j = (size - 1 - dy, size - 1 - j) if flip else (dy, j)
                        total[u] = total[u] + dw_ref[i, j : j + 1, :] * piece
            for u in range(rim):
                col = u if side == 0 else tile - rim + u
                at = pl.ds(col, tile, stride=tile)
                acc[s, at, :] = acc[s, at, :] + total[u]

    def edges_all(buf, flip):
        def one(s, carry):
            edges(s, buf, flip)
            return carry

        lax.fori_loop(0, slots, one, 0)

    def prepare():
        for t in range(depth * depth):
            build_band(1, t)
        for s in range(slots):
            relayout(s)

    centre(False, prepare)
    for copy in x_copies:
        copy.wait()
    edges_all(hx, False)

    strip_rows = 4
    chunk = strip_rows * tile
    small = 64
    nhalf = half * tile

    def pred_copy(s, p):
        return pltpu.make_async_remote_copy(
            src_ref=pmine.at[s],
            dst_ref=pall.at[p - 1, s],
            send_sem=sp.at[p - 1, s],
            recv_sem=rp.at[p - 1, s],
            device_id={"ens": lax.rem(mine + p, members)},
            device_id_type=MESH,
        )

    def forward(s, carry):
        for q in range(tile // strip_rows):
            at = slice(q * chunk, (q + 1) * chunk)
            z = acc[s, at, :] + dwb_ref[...]
            mean = jnp.mean(z, axis=1, keepdims=True)
            z = z - mean
            inv = lax.rsqrt(jnp.mean(z * z, axis=1, keepdims=True) + epsilon)
            z = z * inv
            normed[s, at, :] = z
            invs[s, at, :] = jnp.broadcast_to(inv, (chunk, width))
            feat[at, :] = (z * gain_ref[...] + lnb_ref[...]).astype(bf16)
        for b in range(2):
            base = b * nhalf
            pre[b] = jnp.dot(
                feat[base : base + nhalf, :], win_ref[...], preferred_element_type=f32
            )

            for q in range(nhalf // small):
                at = slice(q * small, (q + 1) * small)
                v = pre[b, at, :] + bin_ref[...]
                cum = 0.5 * (1.0 + lax.erf(v * 0.7071067811865476))
                act[b, at, :] = (v * cum).astype(bf16)
                slope[s, b, at, :] = cum + v * jnp.exp2(v * v * -0.7213475204444817) * 0.3989422804014327
            r16 = lax.dot_general(
                both_hl,
                jnp.concatenate([xm[s, base : base + nhalf, :], act[b]], axis=1),
                NT,
                preferred_element_type=f32,
            )
            r4 = r16[:nv] + r16[nv : 2 * nv] + bias_head
            for q in range(nhalf // width):
                pmine[s, pl.ds(b * (nhalf // width) + q, nv, stride=cells // width), :] = r4[
                    :, q * width : (q + 1) * width
                ]
        for p in range(1, members):
            pred_copy(s, p).start()
        return carry

    lax.fori_loop(0, slots, forward, 0)

    def gz_copy(s, side):
        return edge_copy(eg.at[side, s], hg.at[side, s], sg.at[side, s], rg.at[side, s], side)

    deep = cells // width

    def backward(s, carry):
        for p in range(1, members):
            pred_copy(s, p).wait()
        every = [pmine[s].reshape(nv, deep, width)] + [
            pall[p - 1, s].reshape(nv, deep, width) for p in range(1, members)
        ]
        goal = goals[s]
        mask = masks[s]
        skill = soft_abs(every[0] - goal)
        spread = jnp.zeros_like(skill)
        pull = jnp.zeros_like(skill)
        for p in range(1, members):
            skill = skill + soft_abs(every[p] - goal)
            pull = pull + soft_sign(every[0] - every[p])
            for other in range(p):
                spread = spread + soft_abs(every[p] - every[other])
        same = members * softness**0.5
        score = mask * jnp.sum(
            skill / members - (2.0 * spread + same) / (2 * members * members), axis=0
        )
        for r in range(group):
            piece = pltpu.roll(score, width - r * tile, 1) if r else score
            shuffle[pl.ds(r, tile // group, stride=group), :] = piece
        share = tile // members
        piece = shuffle[pl.ds(pl.multiple_of(mine * share, share), share), :][:, :tile]
        crps_ref[s] = piece.astype(crps_ref.dtype)
        gp = mask[None] * (
            soft_sign(every[0] - goal) / members - pull / (members * members)
        )
        flat[s, 0 : nv * deep, :] = gp.astype(bf16).astype(f32).reshape(nv * deep, width)
        for b in range(2):
            base = b * nhalf
            g4 = jnp.concatenate(
                [
                    flat[s, pl.ds(b * (nhalf // width) + q, nv, stride=deep), :]
                    for q in range(nhalf // width)
                ],
                axis=1,
            )
            gp16 = jnp.concatenate(
                [g4, g4, jnp.zeros((16 - 2 * nv, nhalf), f32)], axis=0
            ).astype(bf16)
            big = lax.dot_general(gp16, both_hl, TN, preferred_element_type=f32)
            grows[s, base : base + nhalf, :] = big[:, :width]
            act[b] = (big[:, width:] * slope[s, b]).astype(bf16)
            full = lax.dot_general(act[b], win_ref[...], NT, preferred_element_type=f32)
            for r in range(half):
                at = slice(base + r * tile, base + (r + 1) * tile)
                g = full[r * tile : (r + 1) * tile] * gain_ref[...]
                z = normed[s, at, :]
                g = invs[s, at, :] * (
                    g
                    - jnp.mean(g, axis=1, keepdims=True)
                    - z * jnp.mean(g * z, axis=1, keepdims=True)
                )
                at = (b * half + r) * wide + LEFT
                pad[s, at : at + tile, :] = g
        strips(s, eg)
        for side in range(2):
            gz_copy(s, side).start()

        return carry

    lax.fori_loop(0, slots, backward, 0)
    centre(True, lambda: None)
    for s in range(slots):
        for side in range(2):
            gz_copy(s, side).wait()

    def last(s, carry):
        edges(s, hg, True)
        v = mcol[s] * (grows[s] + acc[s])
        out_ref[s] = v.reshape(tile, tile, width).astype(bf16)
        return carry

    lax.fori_loop(0, slots, last, 0)


def on_device(
    inputs,
    slot_rows,
    cell_mask,
    target,
    dw_kernel,
    dw_bias,
    ln_gain,
    ln_bias,
    w_in,
    b_in,
    w_out,
    b_out,
    layer_scale,
    w_head,
):
    columns = lax.axis_size("tiles")
    members = lax.axis_size("ens")
    slots, tile, _, width = inputs.shape[3:]
    size = dw_kernel.shape[0]
    rim = size // 2
    half = tile // 2
    cells = tile * tile
    hidden = w_in.shape[1]
    nv = w_head.shape[1]
    vmem = pl.BlockSpec(memory_space=pltpu.VMEM)
    hbm = pl.BlockSpec(memory_space=pl.ANY)
    depth = (size + 1) // 2
    deep = cells // width
    strip = (2, slots, rim, tile, width)
    halo = (2, slots + 1, rim, tile, width)
    dma = pltpu.SemaphoreType.DMA
    operands = [
        slot_rows.T,
        inputs.reshape(slots, tile, tile, width),
        cell_mask.reshape(slots, tile, tile),
        target.reshape(slots, nv, tile, tile),
        dw_kernel,
        dw_bias[None],
        ln_gain[None],
        ln_bias[None],
        w_in,
        b_in[None],
        w_out,
        b_out[None],
        layer_scale[None],
        w_head.T,
    ]
    grad, score = pl.pallas_call(
        functools.partial(kernel, members, columns, slots=slots, tile=tile, size=size, nv=nv),
        out_shape=(
            pltpu.VMEM((slots, tile, tile, width), bf16),
            pltpu.VMEM((slots, tile // members, tile), bf16),
        ),
        in_specs=[hbm] * 14,
        out_specs=(vmem, vmem),
        scratch_shapes=[
            pltpu.VMEM((slots, tile * (tile + 16), width), f32),
            pltpu.VMEM((slots, depth, half + rim, half, 2 * width), bf16),
            pltpu.VMEM((slots, depth, half + rim, half, 2 * width), bf16),
            pltpu.VMEM((2, size + 2, 8, width), f32),
            pltpu.VMEM((depth * depth, 2 * width, 2 * width), bf16),
            pltpu.VMEM((depth * depth, 2 * width, 2 * width), bf16),
            pltpu.VMEM((slots, cells, width), f32),
            pltpu.VMEM((slots, cells, width), f32),
            pltpu.VMEM((slots, cells, width), f32),
            pltpu.VMEM((slots, cells, width), f32),
            pltpu.VMEM((slots, cells, width), f32),
            pltpu.VMEM((slots, cells, width), bf16),
            pltpu.VMEM((cells, width), bf16),
            pltpu.VMEM((2, half * tile, hidden), f32),
            pltpu.VMEM((2, half * tile, hidden), bf16),
            pltpu.VMEM((slots, 2, half * tile, hidden), f32),
            pltpu.VMEM((slots, (nv + 1) * tile, width), f32),
            pltpu.VMEM((slots, nv, deep, width), f32),
            pltpu.VMEM((slots, deep, width), f32),
            pltpu.VMEM((tile, width), f32),
            pltpu.VMEM((2, rim, tile + 16, width), f32),
            pltpu.VMEM(strip, bf16),
            pltpu.VMEM(halo, bf16),
            pltpu.VMEM(strip, bf16),
            pltpu.VMEM(halo, bf16),
            pltpu.VMEM((slots, nv * deep, width), f32),
            pltpu.VMEM((members - 1, slots, nv * deep, width), f32),
            dma((2,)),
            dma((2,)),
            dma((2, slots)),
            dma((2, slots)),
            dma((members - 1, slots)),
            dma((members - 1, slots)),
        ]
        + [
            (pltpu.SMEM if n == 0 else pltpu.VMEM)(a.shape, a.dtype)
            for n, a in enumerate(operands)
        ]
        + [dma((len(operands) + slots - 1,))],
        compiler_params=pltpu.CompilerParams(
            collective_id=0, has_side_effects=True, vmem_limit_bytes=60 * 2**20
        ),
    )(*[pltpu.with_memory_space_constraint(a, pltpu.HBM) for a in operands])
    return (grad.reshape(inputs.shape), score[None, None])


def solution(mesh):
    placed = (
        P("ens", "lev", ("groups", "tiles"), None, None, None, None),
        P("groups", None),
        P("lev", ("groups", "tiles"), None, None, None),
        P("lev", ("groups", "tiles"), None, None, None, None),
    ) + (P(),) * 10
    return jax.shard_map(
        on_device,
        mesh=mesh,
        in_specs=placed,
        out_specs=(
            P("ens", "lev", ("groups", "tiles"), None, None, None, None),
            P("lev", ("groups", "tiles"), None, "ens", None),
        ),
        check_vma=False,
    )
```

```python
import functools

import jax
import jax.numpy as jnp
from jax import lax
from jax.experimental import pallas as pl
from jax.experimental.pallas import tpu as pltpu
from jax.sharding import PartitionSpec as P

softness = 0.0625
epsilon = 1e-06
MESH = pl.DeviceIdType.MESH
f32 = jnp.float32
bf16 = jnp.bfloat16
LEFT = 8
NT = (((1,), (1,)), ((), ()))
TN = (((0,), (0,)), ((), ()))


def soft_abs(value):
    return jnp.sqrt(value * value + softness)


def soft_sign(value):
    return value * lax.rsqrt(value * value + softness)


def kernel(
    members,
    columns,
    rows_hbm,
    x_hbm,
    mask_hbm,
    goal_hbm,
    dw_hbm,
    dwb_hbm,
    gain_hbm,
    lnb_hbm,
    win_hbm,
    bin_hbm,
    wout_hbm,
    bout_hbm,
    ls_hbm,
    wh_hbm,
    out_ref,
    crps_ref,
    pad,
    lhs_lo,
    lhs_hi,
    taps,
    band_lo,
    band_hi,
    acc,
    normed,
    invs,
    grows,
    mcol,
    xm,
    feat,
    pre,
    act,
    slope,
    flat,
    goals,
    masks,
    shuffle,
    halo,
    ex,
    hx,
    eg,
    hg,
    pmine,
    pall,
    sx,
    rx,
    sg,
    rg,
    sp,
    rp,
    rows_ref,
    x_ref,
    mask_ref,
    goal_ref,
    dw_ref,
    dwb_ref,
    gain_ref,
    lnb_ref,
    win_ref,
    bin_ref,
    wout_ref,
    bout_ref,
    ls_ref,
    wh_ref,
    loaded,
    *,
    slots,
    tile,
    size,
    nv,
):
    rim = size // 2
    half = tile // 2
    width = x_ref.shape[-1]
    lanes = width // 2
    cells = tile * tile
    group = width // tile
    depth = (size + 1) // 2
    wide = tile + 16
    lhs = (lhs_lo, lhs_hi)
    band = (band_lo, band_hi)
    me = lax.axis_index("tiles")
    mine = lax.axis_index("ens")
    west = lax.rem(me + columns - 1, columns)
    east = lax.rem(me + 1, columns)

    barrier = pltpu.get_barrier_semaphore()
    pl.semaphore_signal(barrier, inc=1, device_id={"tiles": west}, device_id_type=MESH)
    pl.semaphore_signal(barrier, inc=1, device_id={"tiles": east}, device_id_type=MESH)
    for p in range(1, members):
        pl.semaphore_signal(
            barrier, inc=1, device_id={"ens": lax.rem(mine + p, members)}, device_id_type=MESH
        )

    pairs = [(dw_hbm, dw_ref), (rows_hbm, rows_ref), (mask_hbm, mask_ref)]
    pairs += [(x_hbm.at[s], x_ref.at[s]) for s in range(slots)]
    pairs += [
        (goal_hbm, goal_ref),
        (wh_hbm, wh_ref),
        (ls_hbm, ls_ref),
        (wout_hbm, wout_ref),
        (bout_hbm, bout_ref),
        (dwb_hbm, dwb_ref),
        (gain_hbm, gain_ref),
        (lnb_hbm, lnb_ref),
        (win_hbm, win_ref),
        (bin_hbm, bin_ref),
    ]
    loads = [
        pltpu.make_async_copy(src, dst, loaded.at[n]) for n, (src, dst) in enumerate(pairs)
    ]
    for load in loads:
        load.start()

    zero_strip = jnp.zeros((rim, tile, width), bf16)
    for side in range(2):
        hx[side, slots] = zero_strip
        hg[side, slots] = zero_strip

    eye_tile = (
        lax.broadcasted_iota(jnp.int32, (tile, tile), 0)
        == lax.broadcasted_iota(jnp.int32, (tile, tile), 1)
    ).astype(f32)
    ones = jnp.ones((tile, width), bf16)

    def mask_slot(s, carry):
        pltpu.make_async_copy(x_hbm.at[s], x_ref.at[s], loaded.at[3 + s]).wait()
        live = (rows_ref[s, me] >= 0).astype(f32)
        m = mask_ref[s].astype(f32) * live
        spread = (m[:, None, :] * eye_tile[None]).reshape(cells, tile).astype(bf16)
        col = jnp.dot(spread, ones, preferred_element_type=f32)
        mcol[s] = col
        xv = x_ref[s].astype(f32).reshape(cells, width) * col
        xm[s] = xv.astype(bf16)
        edge = jnp.zeros((LEFT, width), f32)
        for y in range(tile):
            at = y * wide
            pad[s, at : at + LEFT, :] = edge
            pad[s, at + LEFT : at + LEFT + tile, :] = xv[y * tile : (y + 1) * tile]
            pad[s, at + LEFT + tile : at + wide, :] = edge
        return carry

    def relayout(s):
        live = (rows_ref[s, me] >= 0).astype(f32)
        flat[s, nv * tile : (nv + 1) * tile, :tile] = mask_ref[s].astype(f32) * live
        flat[s, 0 : nv * tile, :tile] = goal_ref[s].astype(f32).reshape(nv * tile, tile)
        lane = lax.broadcasted_iota(jnp.int32, (tile // group, width), 1)
        for v in range(nv + 1):
            total = None
            for r in range(group):
                piece = flat[s, pl.ds(v * tile + r, tile // group, stride=group), :]
                if r:
                    piece = pltpu.roll(piece, r * tile, 1)
                total = piece if r == 0 else jnp.where(lane >= r * tile, piece, total)
            if v < nv:
                goals[s, v] = total
            else:
                masks[s] = total

    def strips(s, dst):
        for c in range(rim):
            at = pl.ds(LEFT + tile - rim + c, tile, stride=wide)
            dst[0, s, c] = pad[s, at, :].astype(bf16)
            at = pl.ds(LEFT + c, tile, stride=wide)
            dst[1, s, c] = pad[s, at, :].astype(bf16)

    loads[0].wait()
    low = lax.broadcasted_iota(jnp.int32, (8, width), 1) < lanes
    zero_row = jnp.zeros((1, width), f32)
    for part in range(2):
        taps[part, 0] = jnp.zeros((8, width), f32)
        taps[part, size + 1] = jnp.zeros((8, width), f32)
    for i in range(size):
        now = jnp.concatenate([dw_ref[i], zero_row], axis=0)
        before = jnp.concatenate([zero_row, dw_ref[i]], axis=0)
        taps[0, i + 1] = jnp.where(low, now, pltpu.roll(before, lanes, 1))
        taps[1, i + 1] = jnp.where(low, pltpu.roll(now, lanes, 1), before)

    diagonal = (
        lax.rem(lax.broadcasted_iota(jnp.int32, (lanes, width), 1), lanes)
        == lax.broadcasted_iota(jnp.int32, (lanes, width), 0)
    ).astype(f32).astype(bf16)

    def build_band(part, t):
        dy, dx = t // depth, lax.rem(t, depth)
        for py in range(2):
            for px in range(2):
                for qy in range(2):
                    row = taps[part, 1 + 2 * dy + py - qy, pl.ds(2 * dx + px, 1), :]
                    row = jnp.broadcast_to(row, (16, width)).astype(bf16)
                    for u in range(0, lanes, 16):
                        at = (2 * py + px) * lanes + u
                        band[part][t, at : at + 16, qy * width : (qy + 1) * width] = (
                            row * diagonal[u : u + 16]
                        )

    def build_low(t, carry):
        build_band(0, t)
        return carry

    lax.fori_loop(0, depth * depth, build_low, 0, unroll=4)

    for load in loads[1:3]:
        load.wait()
    lax.fori_loop(0, slots, mask_slot, 0)
    for s in range(slots):
        strips(s, ex)

    pl.semaphore_wait(barrier, 2 + members - 1)

    def edge_copy(src, dst, send, recv, side):
        return pltpu.make_async_remote_copy(
            src_ref=src,
            dst_ref=dst,
            send_sem=send,
            recv_sem=recv,
            device_id={"tiles": east if side == 0 else west},
            device_id_type=MESH,
        )

    x_copies = [
        edge_copy(ex.at[side], hx.at[side, pl.ds(0, slots)], sx.at[side], rx.at[side], side)
        for side in range(2)
    ]
    for copy in x_copies:
        copy.start()

    for load in loads[3 + slots :]:
        load.wait()

    scaled_head = wh_ref[...] * ls_ref[...]
    through_head = lax.dot_general(
        jnp.concatenate([scaled_head, scaled_head], axis=0), wout_ref[...].astype(f32), NT,
        precision=lax.Precision.HIGHEST, preferred_element_type=f32,
    )[:nv]
    bias_head = jnp.sum(scaled_head * bout_ref[...], axis=1, keepdims=True)
    both = jnp.concatenate([wh_ref[...], through_head], axis=1)
    both_hi = both.astype(bf16).astype(f32)
    both_hl = jnp.concatenate(
        [both_hi, both - both_hi, jnp.zeros((16 - 2 * nv, both.shape[1]), f32)], axis=0
    ).astype(bf16)

    half_lane = lax.broadcasted_iota(jnp.int32, (half, width), 1) < lanes

    def swap(first, second):
        lo = jnp.where(half_lane, first, pltpu.roll(second, lanes, 1))
        hi = jnp.where(half_lane, pltpu.roll(first, lanes, 1), second)
        return lo, hi

    def centre(flip, beside):
        own = [rows_ref[s, me] for s in range(slots)]
        res = []
        for part in range(2):
            if part == 1:
                beside()
            for s in range(slots):
                above, below = max(s - 1, 0), min(s + 1, slots - 1)
                flag_up = ((s > 0) & (own[s] >= 0) & (own[above] == own[s] - 1)).astype(f32)
                flag_down = (
                    (s < slots - 1) & (own[below] >= 0) & (own[below] == own[s] + 1)
                ).astype(f32)
                for r in range(tile + 2 * rim):
                    y = r - rim
                    m, py = r // 2, r % 2
                    for dx in range(depth):
                        found = []
                        for px in range(2):
                            at = pl.ds(
                                (y % tile) * wide + LEFT - rim + 2 * dx + px, half, stride=2
                            )
                            if y < 0:
                                piece = pad[above, at, :] * flag_up
                            elif y >= tile:
                                piece = pad[below, at, :] * flag_down
                            else:
                                piece = pad[s, at, :]
                            found.append(piece.astype(bf16))
                        place = py
                        if flip:
                            found = found[::-1]
                            place = 1 - py
                        cut = slice(part * lanes, (part + 1) * lanes)
                        lhs[part][s, dx, m, :, place * width : (place + 1) * width] = (
                            jnp.concatenate([found[0][:, cut], found[1][:, cut]], axis=1)
                        )
            left = []
            right = []
            for dy in range(depth):
                for dx in range(depth):
                    left.append(
                        lhs[part][:, dx, dy : dy + half].reshape(
                            slots * half * half, 2 * width
                        )
                    )
                    oy, ox = (depth - 1 - dy, depth - 1 - dx) if flip else (dy, dx)
                    right.append(band[part][oy * depth + ox])
            res.append(
                jnp.dot(
                    jnp.concatenate(left, axis=1),
                    jnp.concatenate(right, axis=0),
                    preferred_element_type=f32,
                )
            )
        for s in range(slots):
            for qy in range(2):
                y = 1 - qy if flip else qy
                at = slice(qy * width, (qy + 1) * width)
                for k in range(half):
                    base = (s * half + k) * half
                    rows = slice(base, base + half)
                    lo, hi = swap(res[0][rows, at], res[1][rows, at])
                    even, odd = (hi, lo) if flip else (lo, hi)
                    acc[s, pl.ds((2 * k + y) * tile, half, stride=2), :] = even
                    acc[s, pl.ds((2 * k + y) * tile + 1, half, stride=2), :] = odd

    def edges(s, buf, flip):
        row = rows_ref[s, me]
        for side, source in ((0, west), (1, east)):
            there = [rows_ref[t, source] for t in range(slots)]

            def find(wanted):
                place = jnp.int32(slots)
                for t in range(slots):
                    place = jnp.where(
                        (there[t] >= 0) & (there[t] == wanted), jnp.int32(t), place
                    )
                return place

            up = find(row - 1)
            level = find(row)
            down = find(row + 1)
            total = [jnp.zeros((tile, width), f32) for _ in range(rim)]
            for c in range(rim):
                halo[side, c, 0:8] = buf[side, up, c].astype(f32)[tile - 8 :]
                halo[side, c, 8 : 8 + tile] = buf[side, level, c].astype(f32)
                halo[side, c, 8 + tile :] = buf[side, down, c].astype(f32)[:8]
                for dy in range(size):
                    piece = halo[side, c, 8 - rim + dy : 8 - rim + dy + tile]
                    for u in range(rim):
                        if (c < u) if side == 0 else (c > u):
                            continue
                        j = c - u if side == 0 else size - 1 + c - u
                        i, j = (size - 1 - dy, size - 1 - j) if flip else (dy, j)
                        total[u] = total[u] + dw_ref[i, j : j + 1, :] * piece
            for u in range(rim):
                col = u if side == 0 else tile - rim + u
                at = pl.ds(col, tile, stride=tile)
                acc[s, at, :] = acc[s, at, :] + total[u]

    def edges_all(buf, flip):
        def one(s, carry):
            edges(s, buf, flip)
            return carry

        lax.fori_loop(0, slots, one, 0)

    def prepare():
        for t in range(depth * depth):
            build_band(1, t)
        for s in range(slots):
            relayout(s)

    centre(False, prepare)
    for copy in x_copies:
        copy.wait()
    edges_all(hx, False)

    strip_rows = 4
    chunk = strip_rows * tile
    small = 64
    nhalf = half * tile

    def pred_copy(s, p):
        return pltpu.make_async_remote_copy(
            src_ref=pmine.at[s],
            dst_ref=pall.at[p - 1, s],
            send_sem=sp.at[p - 1, s],
            recv_sem=rp.at[p - 1, s],
            device_id={"ens": lax.rem(mine + p, members)},
            device_id_type=MESH,
        )

    def forward(s, carry):
        for q in range(tile // strip_rows):
            at = slice(q * chunk, (q + 1) * chunk)
            z = acc[s, at, :] + dwb_ref[...]
            mean = jnp.mean(z, axis=1, keepdims=True)
            z = z - mean
            inv = lax.rsqrt(jnp.mean(z * z, axis=1, keepdims=True) + epsilon)
            z = z * inv
            normed[s, at, :] = z
            invs[s, at, :] = jnp.broadcast_to(inv, (chunk, width))
            feat[at, :] = (z * gain_ref[...] + lnb_ref[...]).astype(bf16)
        for b in range(2):
            base = b * nhalf
            pre[b] = jnp.dot(
                feat[base : base + nhalf, :], win_ref[...], preferred_element_type=f32
            )

            for q in range(nhalf // small):
                at = slice(q * small, (q + 1) * small)
                v = pre[b, at, :] + bin_ref[...]
                cum = 0.5 * (1.0 + lax.erf(v * 0.7071067811865476))
                act[b, at, :] = (v * cum).astype(bf16)
                slope[s, b, at, :] = cum + v * jnp.exp2(v * v * -0.7213475204444817) * 0.3989422804014327
            r16 = lax.dot_general(
                both_hl,
                jnp.concatenate([xm[s, base : base + nhalf, :], act[b]], axis=1),
                NT,
                preferred_element_type=f32,
            )
            r4 = r16[:nv] + r16[nv : 2 * nv] + bias_head
            for q in range(nhalf // width):
                pmine[s, pl.ds(b * (nhalf // width) + q, nv, stride=cells // width), :] = r4[
                    :, q * width : (q + 1) * width
                ]
        for p in range(1, members):
            pred_copy(s, p).start()
        return carry

    lax.fori_loop(0, slots, forward, 0)

    def gz_copy(s, side):
        return edge_copy(eg.at[side, s], hg.at[side, s], sg.at[side, s], rg.at[side, s], side)

    deep = cells // width

    def backward(s, carry):
        for p in range(1, members):
            pred_copy(s, p).wait()
        every = [pmine[s].reshape(nv, deep, width)] + [
            pall[p - 1, s].reshape(nv, deep, width) for p in range(1, members)
        ]
        goal = goals[s]
        mask = masks[s]
        skill = soft_abs(every[0] - goal)
        spread = jnp.zeros_like(skill)
        pull = jnp.zeros_like(skill)
        for p in range(1, members):
            skill = skill + soft_abs(every[p] - goal)
            pull = pull + soft_sign(every[0] - every[p])
            for other in range(p):
                spread = spread + soft_abs(every[p] - every[other])
        same = members * softness**0.5
        score = mask * jnp.sum(
            skill / members - (2.0 * spread + same) / (2 * members * members), axis=0
        )
        for r in range(group):
            piece = pltpu.roll(score, width - r * tile, 1) if r else score
            shuffle[pl.ds(r, tile // group, stride=group), :] = piece
        share = tile // members
        piece = shuffle[pl.ds(pl.multiple_of(mine * share, share), share), :][:, :tile]
        crps_ref[s] = piece.astype(crps_ref.dtype)
        gp = mask[None] * (
            soft_sign(every[0] - goal) / members - pull / (members * members)
        )
        flat[s, 0 : nv * deep, :] = gp.astype(bf16).astype(f32).reshape(nv * deep, width)
        for b in range(2):
            base = b * nhalf
            g4 = jnp.concatenate(
                [
                    flat[s, pl.ds(b * (nhalf // width) + q, nv, stride=deep), :]
                    for q in range(nhalf // width)
                ],
                axis=1,
            )
            gp16 = jnp.concatenate(
                [g4, g4, jnp.zeros((16 - 2 * nv, nhalf), f32)], axis=0
            ).astype(bf16)
            big = lax.dot_general(gp16, both_hl, TN, preferred_element_type=f32)
            grows[s, base : base + nhalf, :] = big[:, :width]
            act[b] = (big[:, width:] * slope[s, b]).astype(bf16)
            full = lax.dot_general(act[b], win_ref[...], NT, preferred_element_type=f32)
            for r in range(half):
                at = slice(base + r * tile, base + (r + 1) * tile)
                g = full[r * tile : (r + 1) * tile] * gain_ref[...]
                z = normed[s, at, :]
                g = invs[s, at, :] * (
                    g
                    - jnp.mean(g, axis=1, keepdims=True)
                    - z * jnp.mean(g * z, axis=1, keepdims=True)
                )
                at = (b * half + r) * wide + LEFT
                pad[s, at : at + tile, :] = g
        strips(s, eg)
        for side in range(2):
            gz_copy(s, side).start()

        return carry

    lax.fori_loop(0, slots, backward, 0)
    centre(True, lambda: None)
    for s in range(slots):
        for side in range(2):
            gz_copy(s, side).wait()

    def last(s, carry):
        edges(s, hg, True)
        v = mcol[s] * (grows[s] + acc[s])
        out_ref[s] = v.reshape(tile, tile, width).astype(bf16)
        return carry

    lax.fori_loop(0, slots, last, 0)


def store(grad_ref, score_ref, grad_out, score_out, sems):
    copies = [
        pltpu.make_async_copy(grad_ref, grad_out, sems.at[0]),
        pltpu.make_async_copy(score_ref, score_out, sems.at[1]),
    ]
    for copy in copies:
        copy.start()
    for copy in copies:
        copy.wait()


def on_device(
    inputs,
    slot_rows,
    cell_mask,
    target,
    dw_kernel,
    dw_bias,
    ln_gain,
    ln_bias,
    w_in,
    b_in,
    w_out,
    b_out,
    layer_scale,
    w_head,
):
    columns = lax.axis_size("tiles")
    members = lax.axis_size("ens")
    slots, tile, _, width = inputs.shape[3:]
    size = dw_kernel.shape[0]
    rim = size // 2
    half = tile // 2
    cells = tile * tile
    hidden = w_in.shape[1]
    nv = w_head.shape[1]
    vmem = pl.BlockSpec(memory_space=pltpu.VMEM)
    hbm = pl.BlockSpec(memory_space=pl.ANY)
    depth = (size + 1) // 2
    deep = cells // width
    strip = (2, slots, rim, tile, width)
    halo = (2, slots + 1, rim, tile, width)
    dma = pltpu.SemaphoreType.DMA
    operands = [
        slot_rows.T,
        inputs.reshape(slots, tile, tile, width),
        cell_mask.reshape(slots, tile, tile),
        target.reshape(slots, nv, tile, tile),
        dw_kernel,
        dw_bias[None],
        ln_gain[None],
        ln_bias[None],
        w_in,
        b_in[None],
        w_out,
        b_out[None],
        layer_scale[None],
        w_head.T,
    ]
    grad, score = pl.pallas_call(
        functools.partial(kernel, members, columns, slots=slots, tile=tile, size=size, nv=nv),
        out_shape=(
            pltpu.VMEM((slots, tile, tile, width), bf16),
            pltpu.VMEM((slots, tile // members, tile), bf16),
        ),
        in_specs=[hbm] * 14,
        out_specs=(vmem, vmem),
        scratch_shapes=[
            pltpu.VMEM((slots, tile * (tile + 16), width), f32),
            pltpu.VMEM((slots, depth, half + rim, half, 2 * width), bf16),
            pltpu.VMEM((slots, depth, half + rim, half, 2 * width), bf16),
            pltpu.VMEM((2, size + 2, 8, width), f32),
            pltpu.VMEM((depth * depth, 2 * width, 2 * width), bf16),
            pltpu.VMEM((depth * depth, 2 * width, 2 * width), bf16),
            pltpu.VMEM((slots, cells, width), f32),
            pltpu.VMEM((slots, cells, width), f32),
            pltpu.VMEM((slots, cells, width), f32),
            pltpu.VMEM((slots, cells, width), f32),
            pltpu.VMEM((slots, cells, width), f32),
            pltpu.VMEM((slots, cells, width), bf16),
            pltpu.VMEM((cells, width), bf16),
            pltpu.VMEM((2, half * tile, hidden), f32),
            pltpu.VMEM((2, half * tile, hidden), bf16),
            pltpu.VMEM((slots, 2, half * tile, hidden), f32),
            pltpu.VMEM((slots, (nv + 1) * tile, width), f32),
            pltpu.VMEM((slots, nv, deep, width), f32),
            pltpu.VMEM((slots, deep, width), f32),
            pltpu.VMEM((tile, width), f32),
            pltpu.VMEM((2, rim, tile + 16, width), f32),
            pltpu.VMEM(strip, bf16),
            pltpu.VMEM(halo, bf16),
            pltpu.VMEM(strip, bf16),
            pltpu.VMEM(halo, bf16),
            pltpu.VMEM((slots, nv * deep, width), f32),
            pltpu.VMEM((members - 1, slots, nv * deep, width), f32),
            dma((2,)),
            dma((2,)),
            dma((2, slots)),
            dma((2, slots)),
            dma((members - 1, slots)),
            dma((members - 1, slots)),
        ]
        + [
            (pltpu.SMEM if n == 0 else pltpu.VMEM)(a.shape, a.dtype)
            for n, a in enumerate(operands)
        ]
        + [dma((len(operands) + slots - 1,))],
        compiler_params=pltpu.CompilerParams(
            collective_id=0, has_side_effects=True, vmem_limit_bytes=60 * 2**20
        ),
    )(*[pltpu.with_memory_space_constraint(a, pltpu.HBM) for a in operands])
    grad, score = pl.pallas_call(
        store,
        out_shape=(
            jax.ShapeDtypeStruct(grad.shape, grad.dtype),
            jax.ShapeDtypeStruct(score.shape, score.dtype),
        ),
        in_specs=[vmem] * 2,
        out_specs=(hbm, hbm),
        scratch_shapes=[dma((2,))],
    )(
        pltpu.with_memory_space_constraint(grad, pltpu.VMEM),
        pltpu.with_memory_space_constraint(score, pltpu.VMEM),
    )
    return (grad.reshape(inputs.shape), score[None, None])


def solution(mesh):
    placed = (
        P("ens", "lev", ("groups", "tiles"), None, None, None, None),
        P("groups", None),
        P("lev", ("groups", "tiles"), None, None, None),
        P("lev", ("groups", "tiles"), None, None, None, None),
    ) + (P(),) * 10
    return jax.shard_map(
        on_device,
        mesh=mesh,
        in_specs=placed,
        out_specs=(
            P("ens", "lev", ("groups", "tiles"), None, None, None, None),
            P("lev", ("groups", "tiles"), None, "ens", None),
        ),
        check_vma=False,
    )
```

```python
import functools

import jax
import jax.numpy as jnp
from jax import lax
from jax.experimental import pallas as pl
from jax.experimental.pallas import tpu as pltpu
from jax.sharding import PartitionSpec as P

softness = 0.0625
epsilon = 1e-06
MESH = pl.DeviceIdType.MESH
f32 = jnp.float32
bf16 = jnp.bfloat16
LEFT = 8
NT = (((1,), (1,)), ((), ()))
TN = (((0,), (0,)), ((), ()))


def soft_abs(value):
    return jnp.sqrt(value * value + softness)


def soft_sign(value):
    return value * lax.rsqrt(value * value + softness)


def kernel(
    members,
    columns,
    rows_hbm,
    x_hbm,
    mask_hbm,
    goal_hbm,
    dw_hbm,
    dwb_hbm,
    gain_hbm,
    lnb_hbm,
    win_hbm,
    bin_hbm,
    wout_hbm,
    bout_hbm,
    ls_hbm,
    wh_hbm,
    acc,
    grows,
    mcol,
    crps_ref,
    pad,
    lhs_lo,
    lhs_hi,
    taps,
    band_lo,
    band_hi,
    normed,
    invs,
    xm,
    feat,
    pre,
    act,
    slope,
    flat,
    goals,
    masks,
    shuffle,
    halo,
    ex,
    hx,
    eg,
    hg,
    pmine,
    pall,
    sx,
    rx,
    sg,
    rg,
    sp,
    rp,
    rows_ref,
    x_ref,
    mask_ref,
    goal_ref,
    dw_ref,
    dwb_ref,
    gain_ref,
    lnb_ref,
    win_ref,
    bin_ref,
    wout_ref,
    bout_ref,
    ls_ref,
    wh_ref,
    loaded,
    *,
    slots,
    tile,
    size,
    nv,
):
    rim = size // 2
    half = tile // 2
    width = x_ref.shape[-1]
    lanes = width // 2
    cells = tile * tile
    group = width // tile
    depth = (size + 1) // 2
    wide = tile + 16
    lhs = (lhs_lo, lhs_hi)
    band = (band_lo, band_hi)
    me = lax.axis_index("tiles")
    mine = lax.axis_index("ens")
    west = lax.rem(me + columns - 1, columns)
    east = lax.rem(me + 1, columns)

    barrier = pltpu.get_barrier_semaphore()
    pl.semaphore_signal(barrier, inc=1, device_id={"tiles": west}, device_id_type=MESH)
    pl.semaphore_signal(barrier, inc=1, device_id={"tiles": east}, device_id_type=MESH)
    for p in range(1, members):
        pl.semaphore_signal(
            barrier, inc=1, device_id={"ens": lax.rem(mine + p, members)}, device_id_type=MESH
        )

    pairs = [(dw_hbm, dw_ref), (rows_hbm, rows_ref), (mask_hbm, mask_ref)]
    pairs += [(x_hbm.at[s], x_ref.at[s]) for s in range(slots)]
    pairs += [
        (goal_hbm, goal_ref),
        (wh_hbm, wh_ref),
        (ls_hbm, ls_ref),
        (wout_hbm, wout_ref),
        (bout_hbm, bout_ref),
        (dwb_hbm, dwb_ref),
        (gain_hbm, gain_ref),
        (lnb_hbm, lnb_ref),
        (win_hbm, win_ref),
        (bin_hbm, bin_ref),
    ]
    loads = [
        pltpu.make_async_copy(src, dst, loaded.at[n]) for n, (src, dst) in enumerate(pairs)
    ]
    for load in loads:
        load.start()

    zero_strip = jnp.zeros((rim, tile, width), bf16)
    for side in range(2):
        hx[side, slots] = zero_strip
        hg[side, slots] = zero_strip

    eye_tile = (
        lax.broadcasted_iota(jnp.int32, (tile, tile), 0)
        == lax.broadcasted_iota(jnp.int32, (tile, tile), 1)
    ).astype(f32)
    ones = jnp.ones((tile, width), bf16)

    def mask_slot(s, carry):
        pltpu.make_async_copy(x_hbm.at[s], x_ref.at[s], loaded.at[3 + s]).wait()
        live = (rows_ref[s, me] >= 0).astype(f32)
        m = mask_ref[s].astype(f32) * live
        spread = (m[:, None, :] * eye_tile[None]).reshape(cells, tile).astype(bf16)
        col = jnp.dot(spread, ones, preferred_element_type=f32)
        mcol[s] = col
        xv = x_ref[s].astype(f32).reshape(cells, width) * col
        xm[s] = xv.astype(bf16)
        edge = jnp.zeros((LEFT, width), f32)
        for y in range(tile):
            at = y * wide
            pad[s, at : at + LEFT, :] = edge
            pad[s, at + LEFT : at + LEFT + tile, :] = xv[y * tile : (y + 1) * tile]
            pad[s, at + LEFT + tile : at + wide, :] = edge
        return carry

    def relayout(s):
        live = (rows_ref[s, me] >= 0).astype(f32)
        flat[s, nv * tile : (nv + 1) * tile, :tile] = mask_ref[s].astype(f32) * live
        flat[s, 0 : nv * tile, :tile] = goal_ref[s].astype(f32).reshape(nv * tile, tile)
        lane = lax.broadcasted_iota(jnp.int32, (tile // group, width), 1)
        for v in range(nv + 1):
            total = None
            for r in range(group):
                piece = flat[s, pl.ds(v * tile + r, tile // group, stride=group), :]
                if r:
                    piece = pltpu.roll(piece, r * tile, 1)
                total = piece if r == 0 else jnp.where(lane >= r * tile, piece, total)
            if v < nv:
                goals[s, v] = total
            else:
                masks[s] = total

    def strips(s, dst):
        for c in range(rim):
            at = pl.ds(LEFT + tile - rim + c, tile, stride=wide)
            dst[0, s, c] = pad[s, at, :].astype(bf16)
            at = pl.ds(LEFT + c, tile, stride=wide)
            dst[1, s, c] = pad[s, at, :].astype(bf16)

    loads[0].wait()
    low = lax.broadcasted_iota(jnp.int32, (8, width), 1) < lanes
    zero_row = jnp.zeros((1, width), f32)
    for part in range(2):
        taps[part, 0] = jnp.zeros((8, width), f32)
        taps[part, size + 1] = jnp.zeros((8, width), f32)
    for i in range(size):
        now = jnp.concatenate([dw_ref[i], zero_row], axis=0)
        before = jnp.concatenate([zero_row, dw_ref[i]], axis=0)
        taps[0, i + 1] = jnp.where(low, now, pltpu.roll(before, lanes, 1))
        taps[1, i + 1] = jnp.where(low, pltpu.roll(now, lanes, 1), before)

    diagonal = (
        lax.rem(lax.broadcasted_iota(jnp.int32, (lanes, width), 1), lanes)
        == lax.broadcasted_iota(jnp.int32, (lanes, width), 0)
    ).astype(f32).astype(bf16)

    def build_band(part, t):
        dy, dx = t // depth, lax.rem(t, depth)
        for py in range(2):
            for px in range(2):
                for qy in range(2):
                    row = taps[part, 1 + 2 * dy + py - qy, pl.ds(2 * dx + px, 1), :]
                    row = jnp.broadcast_to(row, (16, width)).astype(bf16)
                    for u in range(0, lanes, 16):
                        at = (2 * py + px) * lanes + u
                        band[part][t, at : at + 16, qy * width : (qy + 1) * width] = (
                            row * diagonal[u : u + 16]
                        )

    def build_low(t, carry):
        build_band(0, t)
        return carry

    lax.fori_loop(0, depth * depth, build_low, 0, unroll=4)

    for load in loads[1:3]:
        load.wait()
    lax.fori_loop(0, slots, mask_slot, 0)
    for s in range(slots):
        strips(s, ex)

    pl.semaphore_wait(barrier, 2 + members - 1)

    def edge_copy(src, dst, send, recv, side):
        return pltpu.make_async_remote_copy(
            src_ref=src,
            dst_ref=dst,
            send_sem=send,
            recv_sem=recv,
            device_id={"tiles": east if side == 0 else west},
            device_id_type=MESH,
        )

    x_copies = [
        edge_copy(ex.at[side], hx.at[side, pl.ds(0, slots)], sx.at[side], rx.at[side], side)
        for side in range(2)
    ]
    for copy in x_copies:
        copy.start()

    for load in loads[3 + slots :]:
        load.wait()

    scaled_head = wh_ref[...] * ls_ref[...]
    through_head = lax.dot_general(
        jnp.concatenate([scaled_head, scaled_head], axis=0), wout_ref[...].astype(f32), NT,
        precision=lax.Precision.HIGHEST, preferred_element_type=f32,
    )[:nv]
    bias_head = jnp.sum(scaled_head * bout_ref[...], axis=1, keepdims=True)
    both = jnp.concatenate([wh_ref[...], through_head], axis=1)
    both_hi = both.astype(bf16).astype(f32)
    both_hl = jnp.concatenate(
        [both_hi, both - both_hi, jnp.zeros((16 - 2 * nv, both.shape[1]), f32)], axis=0
    ).astype(bf16)

    half_lane = lax.broadcasted_iota(jnp.int32, (half, width), 1) < lanes

    def swap(first, second):
        lo = jnp.where(half_lane, first, pltpu.roll(second, lanes, 1))
        hi = jnp.where(half_lane, pltpu.roll(first, lanes, 1), second)
        return lo, hi

    def centre(flip, beside):
        own = [rows_ref[s, me] for s in range(slots)]
        res = []
        for part in range(2):
            if part == 1:
                beside()
            for s in range(slots):
                above, below = max(s - 1, 0), min(s + 1, slots - 1)
                flag_up = ((s > 0) & (own[s] >= 0) & (own[above] == own[s] - 1)).astype(f32)
                flag_down = (
                    (s < slots - 1) & (own[below] >= 0) & (own[below] == own[s] + 1)
                ).astype(f32)
                for r in range(tile + 2 * rim):
                    y = r - rim
                    m, py = r // 2, r % 2
                    for dx in range(depth):
                        found = []
                        for px in range(2):
                            at = pl.ds(
                                (y % tile) * wide + LEFT - rim + 2 * dx + px, half, stride=2
                            )
                            if y < 0:
                                piece = pad[above, at, :] * flag_up
                            elif y >= tile:
                                piece = pad[below, at, :] * flag_down
                            else:
                                piece = pad[s, at, :]
                            found.append(piece.astype(bf16))
                        place = py
                        if flip:
                            found = found[::-1]
                            place = 1 - py
                        cut = slice(part * lanes, (part + 1) * lanes)
                        lhs[part][s, dx, m, :, place * width : (place + 1) * width] = (
                            jnp.concatenate([found[0][:, cut], found[1][:, cut]], axis=1)
                        )
            left = []
            right = []
            for dy in range(depth):
                for dx in range(depth):
                    left.append(
                        lhs[part][:, dx, dy : dy + half].reshape(
                            slots * half * half, 2 * width
                        )
                    )
                    oy, ox = (depth - 1 - dy, depth - 1 - dx) if flip else (dy, dx)
                    right.append(band[part][oy * depth + ox])
            res.append(
                jnp.dot(
                    jnp.concatenate(left, axis=1),
                    jnp.concatenate(right, axis=0),
                    preferred_element_type=f32,
                )
            )
        for s in range(slots):
            for qy in range(2):
                y = 1 - qy if flip else qy
                at = slice(qy * width, (qy + 1) * width)
                for k in range(half):
                    base = (s * half + k) * half
                    rows = slice(base, base + half)
                    lo, hi = swap(res[0][rows, at], res[1][rows, at])
                    even, odd = (hi, lo) if flip else (lo, hi)
                    acc[s, pl.ds((2 * k + y) * tile, half, stride=2), :] = even
                    acc[s, pl.ds((2 * k + y) * tile + 1, half, stride=2), :] = odd

    def edges(s, buf, flip):
        row = rows_ref[s, me]
        for side, source in ((0, west), (1, east)):
            there = [rows_ref[t, source] for t in range(slots)]

            def find(wanted):
                place = jnp.int32(slots)
                for t in range(slots):
                    place = jnp.where(
                        (there[t] >= 0) & (there[t] == wanted), jnp.int32(t), place
                    )
                return place

            up = find(row - 1)
            level = find(row)
            down = find(row + 1)
            total = [jnp.zeros((tile, width), f32) for _ in range(rim)]
            for c in range(rim):
                halo[side, c, 0:8] = buf[side, up, c].astype(f32)[tile - 8 :]
                halo[side, c, 8 : 8 + tile] = buf[side, level, c].astype(f32)
                halo[side, c, 8 + tile :] = buf[side, down, c].astype(f32)[:8]
                for dy in range(size):
                    piece = halo[side, c, 8 - rim + dy : 8 - rim + dy + tile]
                    for u in range(rim):
                        if (c < u) if side == 0 else (c > u):
                            continue
                        j = c - u if side == 0 else size - 1 + c - u
                        i, j = (size - 1 - dy, size - 1 - j) if flip else (dy, j)
                        total[u] = total[u] + dw_ref[i, j : j + 1, :] * piece
            for u in range(rim):
                col = u if side == 0 else tile - rim + u
                at = pl.ds(col, tile, stride=tile)
                acc[s, at, :] = acc[s, at, :] + total[u]

    def edges_all(buf, flip):
        def one(s, carry):
            edges(s, buf, flip)
            return carry

        lax.fori_loop(0, slots, one, 0)

    def prepare():
        for t in range(depth * depth):
            build_band(1, t)
        for s in range(slots):
            relayout(s)

    centre(False, prepare)
    for copy in x_copies:
        copy.wait()
    edges_all(hx, False)

    strip_rows = 4
    chunk = strip_rows * tile
    small = 64
    nhalf = half * tile

    def pred_copy(s, p):
        return pltpu.make_async_remote_copy(
            src_ref=pmine.at[s],
            dst_ref=pall.at[p - 1, s],
            send_sem=sp.at[p - 1, s],
            recv_sem=rp.at[p - 1, s],
            device_id={"ens": lax.rem(mine + p, members)},
            device_id_type=MESH,
        )

    def forward(s, carry):
        for q in range(tile // strip_rows):
            at = slice(q * chunk, (q + 1) * chunk)
            z = acc[s, at, :] + dwb_ref[...]
            mean = jnp.mean(z, axis=1, keepdims=True)
            z = z - mean
            inv = lax.rsqrt(jnp.mean(z * z, axis=1, keepdims=True) + epsilon)
            z = z * inv
            normed[s, at, :] = z
            invs[s, at, :] = jnp.broadcast_to(inv, (chunk, width))
            feat[at, :] = (z * gain_ref[...] + lnb_ref[...]).astype(bf16)
        for b in range(2):
            base = b * nhalf
            pre[b] = jnp.dot(
                feat[base : base + nhalf, :], win_ref[...], preferred_element_type=f32
            )

            for q in range(nhalf // small):
                at = slice(q * small, (q + 1) * small)
                v = pre[b, at, :] + bin_ref[...]
                cum = 0.5 * (1.0 + lax.erf(v * 0.7071067811865476))
                act[b, at, :] = (v * cum).astype(bf16)
                slope[s, b, at, :] = cum + v * jnp.exp2(v * v * -0.7213475204444817) * 0.3989422804014327
            r16 = lax.dot_general(
                both_hl,
                jnp.concatenate([xm[s, base : base + nhalf, :], act[b]], axis=1),
                NT,
                preferred_element_type=f32,
            )
            r4 = r16[:nv] + r16[nv : 2 * nv] + bias_head
            for q in range(nhalf // width):
                pmine[s, pl.ds(b * (nhalf // width) + q, nv, stride=cells // width), :] = r4[
                    :, q * width : (q + 1) * width
                ]
        for p in range(1, members):
            pred_copy(s, p).start()
        return carry

    lax.fori_loop(0, slots, forward, 0)

    def gz_copy(s, side):
        return edge_copy(eg.at[side, s], hg.at[side, s], sg.at[side, s], rg.at[side, s], side)

    deep = cells // width

    def backward(s, carry):
        for p in range(1, members):
            pred_copy(s, p).wait()
        every = [pmine[s].reshape(nv, deep, width)] + [
            pall[p - 1, s].reshape(nv, deep, width) for p in range(1, members)
        ]
        goal = goals[s]
        mask = masks[s]
        skill = soft_abs(every[0] - goal)
        spread = jnp.zeros_like(skill)
        pull = jnp.zeros_like(skill)
        for p in range(1, members):
            skill = skill + soft_abs(every[p] - goal)
            pull = pull + soft_sign(every[0] - every[p])
            for other in range(p):
                spread = spread + soft_abs(every[p] - every[other])
        same = members * softness**0.5
        score = mask * jnp.sum(
            skill / members - (2.0 * spread + same) / (2 * members * members), axis=0
        )
        for r in range(group):
            piece = pltpu.roll(score, width - r * tile, 1) if r else score
            shuffle[pl.ds(r, tile // group, stride=group), :] = piece
        share = tile // members
        piece = shuffle[pl.ds(pl.multiple_of(mine * share, share), share), :][:, :tile]
        crps_ref[s] = piece.astype(crps_ref.dtype)
        gp = mask[None] * (
            soft_sign(every[0] - goal) / members - pull / (members * members)
        )
        flat[s, 0 : nv * deep, :] = gp.astype(bf16).astype(f32).reshape(nv * deep, width)
        for b in range(2):
            base = b * nhalf
            g4 = jnp.concatenate(
                [
                    flat[s, pl.ds(b * (nhalf // width) + q, nv, stride=deep), :]
                    for q in range(nhalf // width)
                ],
                axis=1,
            )
            gp16 = jnp.concatenate(
                [g4, g4, jnp.zeros((16 - 2 * nv, nhalf), f32)], axis=0
            ).astype(bf16)
            big = lax.dot_general(gp16, both_hl, TN, preferred_element_type=f32)
            grows[s, base : base + nhalf, :] = big[:, :width]
            act[b] = (big[:, width:] * slope[s, b]).astype(bf16)
            full = lax.dot_general(act[b], win_ref[...], NT, preferred_element_type=f32)
            for r in range(half):
                at = slice(base + r * tile, base + (r + 1) * tile)
                g = full[r * tile : (r + 1) * tile] * gain_ref[...]
                z = normed[s, at, :]
                g = invs[s, at, :] * (
                    g
                    - jnp.mean(g, axis=1, keepdims=True)
                    - z * jnp.mean(g * z, axis=1, keepdims=True)
                )
                at = (b * half + r) * wide + LEFT
                pad[s, at : at + tile, :] = g
        strips(s, eg)
        for side in range(2):
            gz_copy(s, side).start()

        return carry

    lax.fori_loop(0, slots, backward, 0)
    centre(True, lambda: None)
    for s in range(slots):
        for side in range(2):
            gz_copy(s, side).wait()

    def last(s, carry):
        edges(s, hg, True)
        return carry

    lax.fori_loop(0, slots, last, 0)


def store(through, grows, mcol, score_ref, grad_out, score_out, grad_ref, sems):
    slots = grad_ref.shape[0]
    copies = [pltpu.make_async_copy(score_ref, score_out, sems.at[slots])]
    copies[0].start()
    for s in range(slots):
        v = mcol[s] * (grows[s] + through[s])
        grad_ref[s] = v.reshape(grad_ref.shape[1:]).astype(bf16)
        copies.append(pltpu.make_async_copy(grad_ref.at[s], grad_out.at[s], sems.at[s]))
        copies[-1].start()
    for copy in copies:
        copy.wait()


def on_device(
    inputs,
    slot_rows,
    cell_mask,
    target,
    dw_kernel,
    dw_bias,
    ln_gain,
    ln_bias,
    w_in,
    b_in,
    w_out,
    b_out,
    layer_scale,
    w_head,
):
    columns = lax.axis_size("tiles")
    members = lax.axis_size("ens")
    slots, tile, _, width = inputs.shape[3:]
    size = dw_kernel.shape[0]
    rim = size // 2
    half = tile // 2
    cells = tile * tile
    hidden = w_in.shape[1]
    nv = w_head.shape[1]
    vmem = pl.BlockSpec(memory_space=pltpu.VMEM)
    hbm = pl.BlockSpec(memory_space=pl.ANY)
    depth = (size + 1) // 2
    deep = cells // width
    strip = (2, slots, rim, tile, width)
    halo = (2, slots + 1, rim, tile, width)
    dma = pltpu.SemaphoreType.DMA
    operands = [
        slot_rows.T,
        inputs.reshape(slots, tile, tile, width),
        cell_mask.reshape(slots, tile, tile),
        target.reshape(slots, nv, tile, tile),
        dw_kernel,
        dw_bias[None],
        ln_gain[None],
        ln_bias[None],
        w_in,
        b_in[None],
        w_out,
        b_out[None],
        layer_scale[None],
        w_head.T,
    ]
    through, grows, mcol, score = pl.pallas_call(
        functools.partial(kernel, members, columns, slots=slots, tile=tile, size=size, nv=nv),
        out_shape=(
            pltpu.VMEM((slots, cells, width), f32),
            pltpu.VMEM((slots, cells, width), f32),
            pltpu.VMEM((slots, cells, width), f32),
            pltpu.VMEM((slots, tile // members, tile), bf16),
        ),
        in_specs=[hbm] * 14,
        out_specs=(vmem,) * 4,
        scratch_shapes=[
            pltpu.VMEM((slots, tile * (tile + 16), width), f32),
            pltpu.VMEM((slots, depth, half + rim, half, 2 * width), bf16),
            pltpu.VMEM((slots, depth, half + rim, half, 2 * width), bf16),
            pltpu.VMEM((2, size + 2, 8, width), f32),
            pltpu.VMEM((depth * depth, 2 * width, 2 * width), bf16),
            pltpu.VMEM((depth * depth, 2 * width, 2 * width), bf16),
            pltpu.VMEM((slots, cells, width), f32),
            pltpu.VMEM((slots, cells, width), f32),
            pltpu.VMEM((slots, cells, width), bf16),
            pltpu.VMEM((cells, width), bf16),
            pltpu.VMEM((2, half * tile, hidden), f32),
            pltpu.VMEM((2, half * tile, hidden), bf16),
            pltpu.VMEM((slots, 2, half * tile, hidden), f32),
            pltpu.VMEM((slots, (nv + 1) * tile, width), f32),
            pltpu.VMEM((slots, nv, deep, width), f32),
            pltpu.VMEM((slots, deep, width), f32),
            pltpu.VMEM((tile, width), f32),
            pltpu.VMEM((2, rim, tile + 16, width), f32),
            pltpu.VMEM(strip, bf16),
            pltpu.VMEM(halo, bf16),
            pltpu.VMEM(strip, bf16),
            pltpu.VMEM(halo, bf16),
            pltpu.VMEM((slots, nv * deep, width), f32),
            pltpu.VMEM((members - 1, slots, nv * deep, width), f32),
            dma((2,)),
            dma((2,)),
            dma((2, slots)),
            dma((2, slots)),
            dma((members - 1, slots)),
            dma((members - 1, slots)),
        ]
        + [
            (pltpu.SMEM if n == 0 else pltpu.VMEM)(a.shape, a.dtype)
            for n, a in enumerate(operands)
        ]
        + [dma((len(operands) + slots - 1,))],
        compiler_params=pltpu.CompilerParams(
            collective_id=0, has_side_effects=True, vmem_limit_bytes=46 * 2**20
        ),
    )(*[pltpu.with_memory_space_constraint(a, pltpu.HBM) for a in operands])
    grad, score = pl.pallas_call(
        store,
        out_shape=(
            jax.ShapeDtypeStruct((slots, tile, tile, width), bf16),
            jax.ShapeDtypeStruct(score.shape, score.dtype),
        ),
        in_specs=[vmem] * 4,
        out_specs=(hbm, hbm),
        scratch_shapes=[pltpu.VMEM((slots, tile, tile, width), bf16), dma((slots + 1,))],
        compiler_params=pltpu.CompilerParams(vmem_limit_bytes=8 * 2**20),
    )(
        *[
            pltpu.with_memory_space_constraint(a, pltpu.VMEM)
            for a in (through, grows, mcol, score)
        ]
    )
    return (grad.reshape(inputs.shape), score[None, None])


def solution(mesh):
    placed = (
        P("ens", "lev", ("groups", "tiles"), None, None, None, None),
        P("groups", None),
        P("lev", ("groups", "tiles"), None, None, None),
        P("lev", ("groups", "tiles"), None, None, None, None),
    ) + (P(),) * 10
    return jax.shard_map(
        on_device,
        mesh=mesh,
        in_specs=placed,
        out_specs=(
            P("ens", "lev", ("groups", "tiles"), None, None, None, None),
            P("lev", ("groups", "tiles"), None, "ens", None),
        ),
        check_vma=False,
    )
```

```python
import functools

import jax
import jax.numpy as jnp
from jax import lax
from jax.experimental import pallas as pl
from jax.experimental.pallas import tpu as pltpu
from jax.sharding import PartitionSpec as P

softness = 0.0625
epsilon = 1e-06
MESH = pl.DeviceIdType.MESH
f32 = jnp.float32
bf16 = jnp.bfloat16
LEFT = 8
NT = (((1,), (1,)), ((), ()))
TN = (((0,), (0,)), ((), ()))


def soft_abs(value):
    return jnp.sqrt(value * value + softness)


def soft_sign(value):
    return value * lax.rsqrt(value * value + softness)


def kernel(
    members,
    columns,
    rows_hbm,
    x_hbm,
    mask_hbm,
    goal_hbm,
    dw_hbm,
    dwb_hbm,
    gain_hbm,
    lnb_hbm,
    win_hbm,
    bin_hbm,
    wout_hbm,
    bout_hbm,
    ls_hbm,
    wh_hbm,
    acc,
    grows,
    mcol,
    crps_ref,
    pad,
    lhs_lo,
    lhs_hi,
    taps,
    band_lo,
    band_hi,
    normed,
    invs,
    xm,
    feat,
    pre,
    act,
    slope,
    flat,
    goals,
    masks,
    shuffle,
    halo,
    ex,
    hx,
    eg,
    hg,
    pmine,
    pall,
    sx,
    rx,
    sg,
    rg,
    sp,
    rp,
    rows_ref,
    x_ref,
    mask_ref,
    goal_ref,
    dw_ref,
    dwb_ref,
    gain_ref,
    lnb_ref,
    win_ref,
    bin_ref,
    wout_ref,
    bout_ref,
    ls_ref,
    wh_ref,
    loaded,
    *,
    slots,
    tile,
    size,
    nv,
):
    rim = size // 2
    half = tile // 2
    width = x_ref.shape[-1]
    lanes = width // 2
    cells = tile * tile
    group = width // tile
    depth = (size + 1) // 2
    wide = tile + 16
    lhs = (lhs_lo, lhs_hi)
    band = (band_lo, band_hi)
    me = lax.axis_index("tiles")
    mine = lax.axis_index("ens")
    west = lax.rem(me + columns - 1, columns)
    east = lax.rem(me + 1, columns)

    barrier = pltpu.get_barrier_semaphore()
    pl.semaphore_signal(barrier, inc=1, device_id={"tiles": west}, device_id_type=MESH)
    pl.semaphore_signal(barrier, inc=1, device_id={"tiles": east}, device_id_type=MESH)
    for p in range(1, members):
        pl.semaphore_signal(
            barrier, inc=1, device_id={"ens": lax.rem(mine + p, members)}, device_id_type=MESH
        )

    pairs = [(dw_hbm, dw_ref), (rows_hbm, rows_ref), (mask_hbm, mask_ref)]
    pairs += [(x_hbm.at[s], x_ref.at[s]) for s in range(slots)]
    pairs += [
        (goal_hbm, goal_ref),
        (wh_hbm, wh_ref),
        (ls_hbm, ls_ref),
        (wout_hbm, wout_ref),
        (bout_hbm, bout_ref),
        (dwb_hbm, dwb_ref),
        (gain_hbm, gain_ref),
        (lnb_hbm, lnb_ref),
        (win_hbm, win_ref),
        (bin_hbm, bin_ref),
    ]
    loads = [
        pltpu.make_async_copy(src, dst, loaded.at[n]) for n, (src, dst) in enumerate(pairs)
    ]
    for load in loads:
        load.start()

    zero_strip = jnp.zeros((rim, tile, width), bf16)
    for side in range(2):
        hx[side, slots] = zero_strip
        hg[side, slots] = zero_strip

    eye_tile = (
        lax.broadcasted_iota(jnp.int32, (tile, tile), 0)
        == lax.broadcasted_iota(jnp.int32, (tile, tile), 1)
    ).astype(f32)
    ones = jnp.ones((tile, width), bf16)

    def mask_slot(s, carry):
        pltpu.make_async_copy(x_hbm.at[s], x_ref.at[s], loaded.at[3 + s]).wait()
        live = (rows_ref[s, me] >= 0).astype(f32)
        m = mask_ref[s].astype(f32) * live
        spread = (m[:, None, :] * eye_tile[None]).reshape(cells, tile).astype(bf16)
        col = jnp.dot(spread, ones, preferred_element_type=f32)
        mcol[s] = col
        xv = x_ref[s].astype(f32).reshape(cells, width) * col
        xm[s] = xv.astype(bf16)
        edge = jnp.zeros((LEFT, width), f32)
        for y in range(tile):
            at = y * wide
            pad[s, at : at + LEFT, :] = edge
            pad[s, at + LEFT : at + LEFT + tile, :] = xv[y * tile : (y + 1) * tile]
            pad[s, at + LEFT + tile : at + wide, :] = edge
        return carry

    def relayout(s):
        live = (rows_ref[s, me] >= 0).astype(f32)
        flat[s, nv * tile : (nv + 1) * tile, :tile] = mask_ref[s].astype(f32) * live
        flat[s, 0 : nv * tile, :tile] = goal_ref[s].astype(f32).reshape(nv * tile, tile)
        lane = lax.broadcasted_iota(jnp.int32, (tile // group, width), 1)
        for v in range(nv + 1):
            total = None
            for r in range(group):
                piece = flat[s, pl.ds(v * tile + r, tile // group, stride=group), :]
                if r:
                    piece = pltpu.roll(piece, r * tile, 1)
                total = piece if r == 0 else jnp.where(lane >= r * tile, piece, total)
            if v < nv:
                goals[s, v] = total
            else:
                masks[s] = total

    def strips(s, dst):
        for c in range(rim):
            at = pl.ds(LEFT + tile - rim + c, tile, stride=wide)
            dst[0, s, c] = pad[s, at, :].astype(bf16)
            at = pl.ds(LEFT + c, tile, stride=wide)
            dst[1, s, c] = pad[s, at, :].astype(bf16)

    loads[0].wait()
    low = lax.broadcasted_iota(jnp.int32, (8, width), 1) < lanes
    zero_row = jnp.zeros((1, width), f32)
    for part in range(2):
        taps[part, 0] = jnp.zeros((8, width), f32)
        taps[part, size + 1] = jnp.zeros((8, width), f32)
    for i in range(size):
        now = jnp.concatenate([dw_ref[i], zero_row], axis=0)
        before = jnp.concatenate([zero_row, dw_ref[i]], axis=0)
        taps[0, i + 1] = jnp.where(low, now, pltpu.roll(before, lanes, 1))
        taps[1, i + 1] = jnp.where(low, pltpu.roll(now, lanes, 1), before)

    diagonal = (
        lax.rem(lax.broadcasted_iota(jnp.int32, (lanes, width), 1), lanes)
        == lax.broadcasted_iota(jnp.int32, (lanes, width), 0)
    ).astype(f32).astype(bf16)

    def build_band(part, t):
        dy, dx = t // depth, lax.rem(t, depth)
        for py in range(2):
            for px in range(2):
                for qy in range(2):
                    row = taps[part, 1 + 2 * dy + py - qy, pl.ds(2 * dx + px, 1), :]
                    row = jnp.broadcast_to(row, (16, width)).astype(bf16)
                    for u in range(0, lanes, 16):
                        at = (2 * py + px) * lanes + u
                        band[part][t, at : at + 16, qy * width : (qy + 1) * width] = (
                            row * diagonal[u : u + 16]
                        )

    def build_low(t, carry):
        build_band(0, t)
        return carry

    lax.fori_loop(0, depth * depth, build_low, 0, unroll=4)

    for load in loads[1:3]:
        load.wait()
    lax.fori_loop(0, slots, mask_slot, 0)
    for s in range(slots):
        strips(s, ex)

    pl.semaphore_wait(barrier, 2 + members - 1)

    def edge_copy(src, dst, send, recv, side):
        return pltpu.make_async_remote_copy(
            src_ref=src,
            dst_ref=dst,
            send_sem=send,
            recv_sem=recv,
            device_id={"tiles": east if side == 0 else west},
            device_id_type=MESH,
        )

    x_copies = [
        edge_copy(ex.at[side], hx.at[side, pl.ds(0, slots)], sx.at[side], rx.at[side], side)
        for side in range(2)
    ]
    for copy in x_copies:
        copy.start()

    for load in loads[3 + slots :]:
        load.wait()

    scaled_head = wh_ref[...] * ls_ref[...]
    through_head = lax.dot_general(
        jnp.concatenate([scaled_head, scaled_head], axis=0), wout_ref[...].astype(f32), NT,
        precision=lax.Precision.HIGHEST, preferred_element_type=f32,
    )[:nv]
    bias_head = jnp.sum(scaled_head * bout_ref[...], axis=1, keepdims=True)
    both = jnp.concatenate([wh_ref[...], through_head], axis=1)
    both_hi = both.astype(bf16).astype(f32)
    both_hl = jnp.concatenate(
        [both_hi, both - both_hi, jnp.zeros((16 - 2 * nv, both.shape[1]), f32)], axis=0
    ).astype(bf16)

    half_lane = lax.broadcasted_iota(jnp.int32, (half, width), 1) < lanes

    def swap(first, second):
        lo = jnp.where(half_lane, first, pltpu.roll(second, lanes, 1))
        hi = jnp.where(half_lane, pltpu.roll(first, lanes, 1), second)
        return lo, hi

    def centre(flip, beside):
        own = [rows_ref[s, me] for s in range(slots)]
        res = []
        for part in range(2):
            if part == 1:
                beside()
            for s in range(slots):
                above, below = max(s - 1, 0), min(s + 1, slots - 1)
                flag_up = ((s > 0) & (own[s] >= 0) & (own[above] == own[s] - 1)).astype(f32)
                flag_down = (
                    (s < slots - 1) & (own[below] >= 0) & (own[below] == own[s] + 1)
                ).astype(f32)
                for r in range(tile + 2 * rim):
                    y = r - rim
                    m, py = r // 2, r % 2
                    for dx in range(depth):
                        found = []
                        for px in range(2):
                            at = pl.ds(
                                (y % tile) * wide + LEFT - rim + 2 * dx + px, half, stride=2
                            )
                            if y < 0:
                                piece = pad[above, at, :] * flag_up
                            elif y >= tile:
                                piece = pad[below, at, :] * flag_down
                            else:
                                piece = pad[s, at, :]
                            found.append(piece.astype(bf16))
                        place = py
                        if flip:
                            found = found[::-1]
                            place = 1 - py
                        cut = slice(part * lanes, (part + 1) * lanes)
                        lhs[part][s, dx, m, :, place * width : (place + 1) * width] = (
                            jnp.concatenate([found[0][:, cut], found[1][:, cut]], axis=1)
                        )
            left = []
            right = []
            for dy in range(depth):
                for dx in range(depth):
                    left.append(
                        lhs[part][:, dx, dy : dy + half].reshape(
                            slots * half * half, 2 * width
                        )
                    )
                    oy, ox = (depth - 1 - dy, depth - 1 - dx) if flip else (dy, dx)
                    right.append(band[part][oy * depth + ox])
            res.append(
                jnp.dot(
                    jnp.concatenate(left, axis=1),
                    jnp.concatenate(right, axis=0),
                    preferred_element_type=f32,
                )
            )
        for s in range(slots):
            for qy in range(2):
                y = 1 - qy if flip else qy
                at = slice(qy * width, (qy + 1) * width)
                for k in range(half):
                    base = (s * half + k) * half
                    rows = slice(base, base + half)
                    lo, hi = swap(res[0][rows, at], res[1][rows, at])
                    even, odd = (hi, lo) if flip else (lo, hi)
                    acc[s, pl.ds((2 * k + y) * tile, half, stride=2), :] = even
                    acc[s, pl.ds((2 * k + y) * tile + 1, half, stride=2), :] = odd

    def edges(s, buf, flip):
        row = rows_ref[s, me]
        for side, source in ((0, west), (1, east)):
            there = [rows_ref[t, source] for t in range(slots)]

            def find(wanted):
                place = jnp.int32(slots)
                for t in range(slots):
                    place = jnp.where(
                        (there[t] >= 0) & (there[t] == wanted), jnp.int32(t), place
                    )
                return place

            up = find(row - 1)
            level = find(row)
            down = find(row + 1)
            total = [jnp.zeros((tile, width), f32) for _ in range(rim)]
            for c in range(rim):
                halo[s, side, c, 0:8] = buf[side, up, c].astype(f32)[tile - 8 :]
                halo[s, side, c, 8 : 8 + tile] = buf[side, level, c].astype(f32)
                halo[s, side, c, 8 + tile :] = buf[side, down, c].astype(f32)[:8]
                for dy in range(size):
                    piece = halo[s, side, c, 8 - rim + dy : 8 - rim + dy + tile]
                    for u in range(rim):
                        if (c < u) if side == 0 else (c > u):
                            continue
                        j = c - u if side == 0 else size - 1 + c - u
                        i, j = (size - 1 - dy, size - 1 - j) if flip else (dy, j)
                        total[u] = total[u] + dw_ref[i, j : j + 1, :] * piece
            for u in range(rim):
                col = u if side == 0 else tile - rim + u
                at = pl.ds(col, tile, stride=tile)
                acc[s, at, :] = acc[s, at, :] + total[u]

    def edges_all(buf, flip):
        for s in range(slots):
            edges(s, buf, flip)

    def prepare():
        for t in range(depth * depth):
            build_band(1, t)
        for s in range(slots):
            relayout(s)

    centre(False, prepare)
    for copy in x_copies:
        copy.wait()
    edges_all(hx, False)

    strip_rows = 4
    chunk = strip_rows * tile
    small = 64
    nhalf = half * tile

    def pred_copy(s, p):
        return pltpu.make_async_remote_copy(
            src_ref=pmine.at[s],
            dst_ref=pall.at[p - 1, s],
            send_sem=sp.at[p - 1, s],
            recv_sem=rp.at[p - 1, s],
            device_id={"ens": lax.rem(mine + p, members)},
            device_id_type=MESH,
        )

    def forward(s, carry):
        for q in range(tile // strip_rows):
            at = slice(q * chunk, (q + 1) * chunk)
            z = acc[s, at, :] + dwb_ref[...]
            mean = jnp.mean(z, axis=1, keepdims=True)
            z = z - mean
            inv = lax.rsqrt(jnp.mean(z * z, axis=1, keepdims=True) + epsilon)
            z = z * inv
            normed[s, at, :] = z
            invs[s, at, :] = jnp.broadcast_to(inv, (chunk, width))
            feat[at, :] = (z * gain_ref[...] + lnb_ref[...]).astype(bf16)
        for b in range(2):
            base = b * nhalf
            pre[b] = jnp.dot(
                feat[base : base + nhalf, :], win_ref[...], preferred_element_type=f32
            )

            for q in range(nhalf // small):
                at = slice(q * small, (q + 1) * small)
                v = pre[b, at, :] + bin_ref[...]
                cum = 0.5 * (1.0 + lax.erf(v * 0.7071067811865476))
                act[b, at, :] = (v * cum).astype(bf16)
                slope[s, b, at, :] = cum + v * jnp.exp2(v * v * -0.7213475204444817) * 0.3989422804014327
            r16 = lax.dot_general(
                both_hl,
                jnp.concatenate([xm[s, base : base + nhalf, :], act[b]], axis=1),
                NT,
                preferred_element_type=f32,
            )
            r4 = r16[:nv] + r16[nv : 2 * nv] + bias_head
            for q in range(nhalf // width):
                pmine[s, pl.ds(b * (nhalf // width) + q, nv, stride=cells // width), :] = r4[
                    :, q * width : (q + 1) * width
                ]
        for p in range(1, members):
            pred_copy(s, p).start()
        return carry

    lax.fori_loop(0, slots, forward, 0)

    def gz_copy(s, side):
        return edge_copy(eg.at[side, s], hg.at[side, s], sg.at[side, s], rg.at[side, s], side)

    deep = cells // width

    def backward(s, carry):
        for p in range(1, members):
            pred_copy(s, p).wait()
        every = [pmine[s].reshape(nv, deep, width)] + [
            pall[p - 1, s].reshape(nv, deep, width) for p in range(1, members)
        ]
        goal = goals[s]
        mask = masks[s]
        skill = soft_abs(every[0] - goal)
        spread = jnp.zeros_like(skill)
        pull = jnp.zeros_like(skill)
        for p in range(1, members):
            skill = skill + soft_abs(every[p] - goal)
            pull = pull + soft_sign(every[0] - every[p])
            for other in range(p):
                spread = spread + soft_abs(every[p] - every[other])
        same = members * softness**0.5
        score = mask * jnp.sum(
            skill / members - (2.0 * spread + same) / (2 * members * members), axis=0
        )
        for r in range(group):
            piece = pltpu.roll(score, width - r * tile, 1) if r else score
            shuffle[pl.ds(r, tile // group, stride=group), :] = piece
        share = tile // members
        piece = shuffle[pl.ds(pl.multiple_of(mine * share, share), share), :][:, :tile]
        crps_ref[s] = piece.astype(crps_ref.dtype)
        gp = mask[None] * (
            soft_sign(every[0] - goal) / members - pull / (members * members)
        )
        flat[s, 0 : nv * deep, :] = gp.astype(bf16).astype(f32).reshape(nv * deep, width)
        for b in range(2):
            base = b * nhalf
            g4 = jnp.concatenate(
                [
                    flat[s, pl.ds(b * (nhalf // width) + q, nv, stride=deep), :]
                    for q in range(nhalf // width)
                ],
                axis=1,
            )
            gp16 = jnp.concatenate(
                [g4, g4, jnp.zeros((16 - 2 * nv, nhalf), f32)], axis=0
            ).astype(bf16)
            big = lax.dot_general(gp16, both_hl, TN, preferred_element_type=f32)
            grows[s, base : base + nhalf, :] = big[:, :width]
            act[b] = (big[:, width:] * slope[s, b]).astype(bf16)
            full = lax.dot_general(act[b], win_ref[...], NT, preferred_element_type=f32)
            for r in range(half):
                at = slice(base + r * tile, base + (r + 1) * tile)
                g = full[r * tile : (r + 1) * tile] * gain_ref[...]
                z = normed[s, at, :]
                g = invs[s, at, :] * (
                    g
                    - jnp.mean(g, axis=1, keepdims=True)
                    - z * jnp.mean(g * z, axis=1, keepdims=True)
                )
                at = (b * half + r) * wide + LEFT
                pad[s, at : at + tile, :] = g
        strips(s, eg)
        for side in range(2):
            gz_copy(s, side).start()

        return carry

    lax.fori_loop(0, slots, backward, 0)
    centre(True, lambda: None)
    for s in range(slots):
        for side in range(2):
            gz_copy(s, side).wait()

    edges_all(hg, True)


def store(through, grows, mcol, score_ref, grad_out, score_out, grad_ref, sems):
    slots = grad_ref.shape[0]
    copies = [pltpu.make_async_copy(score_ref, score_out, sems.at[slots])]
    copies[0].start()
    for s in range(slots):
        v = mcol[s] * (grows[s] + through[s])
        grad_ref[s] = v.reshape(grad_ref.shape[1:]).astype(bf16)
        copies.append(pltpu.make_async_copy(grad_ref.at[s], grad_out.at[s], sems.at[s]))
        copies[-1].start()
    for copy in copies:
        copy.wait()


def on_device(
    inputs,
    slot_rows,
    cell_mask,
    target,
    dw_kernel,
    dw_bias,
    ln_gain,
    ln_bias,
    w_in,
    b_in,
    w_out,
    b_out,
    layer_scale,
    w_head,
):
    columns = lax.axis_size("tiles")
    members = lax.axis_size("ens")
    slots, tile, _, width = inputs.shape[3:]
    size = dw_kernel.shape[0]
    rim = size // 2
    half = tile // 2
    cells = tile * tile
    hidden = w_in.shape[1]
    nv = w_head.shape[1]
    vmem = pl.BlockSpec(memory_space=pltpu.VMEM)
    hbm = pl.BlockSpec(memory_space=pl.ANY)
    depth = (size + 1) // 2
    deep = cells // width
    strip = (2, slots, rim, tile, width)
    halo = (2, slots + 1, rim, tile, width)
    dma = pltpu.SemaphoreType.DMA
    operands = [
        slot_rows.T,
        inputs.reshape(slots, tile, tile, width),
        cell_mask.reshape(slots, tile, tile),
        target.reshape(slots, nv, tile, tile),
        dw_kernel,
        dw_bias[None],
        ln_gain[None],
        ln_bias[None],
        w_in,
        b_in[None],
        w_out,
        b_out[None],
        layer_scale[None],
        w_head.T,
    ]
    through, grows, mcol, score = pl.pallas_call(
        functools.partial(kernel, members, columns, slots=slots, tile=tile, size=size, nv=nv),
        out_shape=(
            pltpu.VMEM((slots, cells, width), f32),
            pltpu.VMEM((slots, cells, width), f32),
            pltpu.VMEM((slots, cells, width), f32),
            pltpu.VMEM((slots, tile // members, tile), bf16),
        ),
        in_specs=[hbm] * 14,
        out_specs=(vmem,) * 4,
        scratch_shapes=[
            pltpu.VMEM((slots, tile * (tile + 16), width), f32),
            pltpu.VMEM((slots, depth, half + rim, half, 2 * width), bf16),
            pltpu.VMEM((slots, depth, half + rim, half, 2 * width), bf16),
            pltpu.VMEM((2, size + 2, 8, width), f32),
            pltpu.VMEM((depth * depth, 2 * width, 2 * width), bf16),
            pltpu.VMEM((depth * depth, 2 * width, 2 * width), bf16),
            pltpu.VMEM((slots, cells, width), f32),
            pltpu.VMEM((slots, cells, width), f32),
            pltpu.VMEM((slots, cells, width), bf16),
            pltpu.VMEM((cells, width), bf16),
            pltpu.VMEM((2, half * tile, hidden), f32),
            pltpu.VMEM((2, half * tile, hidden), bf16),
            pltpu.VMEM((slots, 2, half * tile, hidden), f32),
            pltpu.VMEM((slots, (nv + 1) * tile, width), f32),
            pltpu.VMEM((slots, nv, deep, width), f32),
            pltpu.VMEM((slots, deep, width), f32),
            pltpu.VMEM((tile, width), f32),
            pltpu.VMEM((slots, 2, rim, tile + 16, width), f32),
            pltpu.VMEM(strip, bf16),
            pltpu.VMEM(halo, bf16),
            pltpu.VMEM(strip, bf16),
            pltpu.VMEM(halo, bf16),
            pltpu.VMEM((slots, nv * deep, width), f32),
            pltpu.VMEM((members - 1, slots, nv * deep, width), f32),
            dma((2,)),
            dma((2,)),
            dma((2, slots)),
            dma((2, slots)),
            dma((members - 1, slots)),
            dma((members - 1, slots)),
        ]
        + [
            (pltpu.SMEM if n == 0 else pltpu.VMEM)(a.shape, a.dtype)
            for n, a in enumerate(operands)
        ]
        + [dma((len(operands) + slots - 1,))],
        compiler_params=pltpu.CompilerParams(
            collective_id=0, has_side_effects=True, vmem_limit_bytes=46 * 2**20
        ),
    )(*[pltpu.with_memory_space_constraint(a, pltpu.HBM) for a in operands])
    grad, score = pl.pallas_call(
        store,
        out_shape=(
            jax.ShapeDtypeStruct((slots, tile, tile, width), bf16),
            jax.ShapeDtypeStruct(score.shape, score.dtype),
        ),
        in_specs=[vmem] * 4,
        out_specs=(hbm, hbm),
        scratch_shapes=[pltpu.VMEM((slots, tile, tile, width), bf16), dma((slots + 1,))],
        compiler_params=pltpu.CompilerParams(vmem_limit_bytes=8 * 2**20),
    )(
        *[
            pltpu.with_memory_space_constraint(a, pltpu.VMEM)
            for a in (through, grows, mcol, score)
        ]
    )
    return (grad.reshape(inputs.shape), score[None, None])


def solution(mesh):
    placed = (
        P("ens", "lev", ("groups", "tiles"), None, None, None, None),
        P("groups", None),
        P("lev", ("groups", "tiles"), None, None, None),
        P("lev", ("groups", "tiles"), None, None, None, None),
    ) + (P(),) * 10
    return jax.shard_map(
        on_device,
        mesh=mesh,
        in_specs=placed,
        out_specs=(
            P("ens", "lev", ("groups", "tiles"), None, None, None, None),
            P("lev", ("groups", "tiles"), None, "ens", None),
        ),
        check_vma=False,
    )
```
